32 devices in a mesh: grp: 4 (over z), gx: 2 (over y), gy: 4 (over x, core).
Axes of the slice: x: 2, y: 2, z: 4, core: 2. Of those that a mesh axis runs over, the one named last changes fastest.
Arguments:
- checkpoint: float32 [2, 2, 2, 32, 64, 256], P(None, None, None, 'gx', 'gy'), may hold values from -6 to 6
- courant: float32 [32, 64, 256], P('gx', 'gy'), may hold values from 0.03 to 0.15
- epsilon: float32 [32, 64, 256], P('gx', 'gy'), may hold values from 0.3 to 0.6
- delta: float32 [32, 64, 256], P('gx', 'gy'), may hold values from 0.05 to 0.3
- positions: int32 [4, 3, 512], replicated, may hold values from 0 to 255, as said below
- amplitudes: float32 [4, 16, 512], replicated, may hold values from -6 to 6
- offsets: int32 [16], replicated, may hold values from -8 to 8, as said below
Outputs:
- image: float32 [16, 32, 64, 256], P('grp', 'gx', 'gy')
The draws below stay inside these ranges and needn't reach their ends.
Inputs may be any that keep to these rules, and one draw needn't show every extreme that they name: `positions`: each column of a row is a cell inside the grid: x below 32, y below 64, z below 256. `offsets`: both -8 and 8 occur.
All inputs are finite; a program needn't handle non-finite values.
Results may differ from the reference program's by a relative error of at most 0.0003.
Values sent between devices are 32-bit elements; how exact they have to be, the bound alone decides.
A program may use at most 128 MiB of HBM per device.

```python
import math
import jax
import jax.numpy as jnp
from jax import lax

NZ = 256
NREC = 512
NSTEPS = 16
SNAP = 4
HMAX = 8
NH = 16
GROUPS = 4
SHOTS = 2
NX = 32
NY = 64


def draw_positions(key, part):
    key_x, key_y, key_z = jax.random.split(jax.random.fold_in(key, 11), 3)
    shape = (GROUPS, NREC)
    coord_x = jax.random.randint(key_x, shape, 0, NX)
    coord_y = jax.random.randint(key_y, shape, 0, NY)
    coord_z = jax.random.randint(key_z, shape, 0, NZ)
    return jnp.stack([coord_x, coord_y, coord_z], 1).astype(jnp.int32)


def draw_offsets(key, part):
    key_vals, key_perm = jax.random.split(jax.random.fold_in(key, 23))
    values = jax.random.randint(key_vals, (NH,), -HMAX, HMAX + 1)
    order = jax.random.permutation(key_perm, NH)
    values = values.at[order[0]].set(HMAX).at[order[1]].set(-HMAX)
    return values.astype(jnp.int32)


def levels(rng, dims, cuts, low, high):
    level, own = 1.0, jax.random.fold_in(rng, 6)
    for dim, parts in cuts:
        steps = jnp.exp(jax.random.uniform(jax.random.fold_in(own, dim), (parts,), jnp.float32, low / len(cuts), high / len(cuts)))
        level = level * jnp.repeat(steps, dims[dim] // parts).reshape([-1 if axis == dim else 1 for axis in range(len(dims))])
    return level


def noise(own_key, dims, width, limit, cuts=(), dtype=jnp.bfloat16):
    factor_of = levels(own_key, dims, cuts, -0.22, 0.18) if cuts else 1.0
    entries = jax.random.normal(own_key, dims, jnp.float32) * width * factor_of
    return jnp.minimum(jnp.maximum(entries, -limit), limit).astype(dtype)


def setup_inputs(seed: int = 0) -> dict:
    streams_of = jax.random.split(jax.random.key(seed), 8)
    checkpoint = noise(streams_of[0], (SHOTS, 2, 2, NX, NY, NZ), 1.0, 6.0, ((3, 2), (4, 4)), jnp.float32)
    courant = jnp.clip(jnp.exp(math.log(0.15) - 1.609438 * jax.random.uniform(streams_of[1], (NX, NY, NZ), jnp.float32) ** levels(streams_of[1], (NX, NY, NZ), ((0, 2), (1, 4)), -0.2, 0.2)), 0.03, 0.15)
    epsilon = jnp.clip(0.3 + 0.3 * jax.random.uniform(streams_of[2], (NX, NY, NZ), jnp.float32) ** levels(streams_of[2], (NX, NY, NZ), ((0, 2), (1, 4)), -0.2, 0.2), 0.3, 0.6)
    delta = jnp.clip(0.05 + 0.25 * jax.random.uniform(streams_of[3], (NX, NY, NZ), jnp.float32) ** levels(streams_of[3], (NX, NY, NZ), ((0, 2), (1, 4)), -0.2, 0.2), 0.05, 0.3)
    positions = draw_positions(jax.random.fold_in(streams_of[7], 71), 0)
    amplitudes = noise(streams_of[5], (GROUPS, NSTEPS, NREC), 1.0, 6.0, (), jnp.float32)
    offsets = draw_offsets(jax.random.fold_in(streams_of[7], 71), 0)
    return dict(checkpoint=checkpoint, courant=courant, epsilon=epsilon, delta=delta, positions=positions, amplitudes=amplitudes, offsets=offsets)


def laplacians(main_field, aux_field):
    padded = jnp.pad(main_field, ((1, 1), (1, 1), (0, 0)))
    across = padded[2:, 1:-1] + padded[:-2, 1:-1] + padded[1:-1, 2:] + padded[1:-1, :-2] - 4.0 * main_field
    deep_pad = jnp.pad(aux_field, ((0, 0), (0, 0), (1, 1)))
    vertical = deep_pad[:, :, 2:] + deep_pad[:, :, :-2] - 2.0 * aux_field
    return (across, vertical)

def replay(current, previous, coefs, coords, strengths):
    flat_index = ((coords[0] * NY + coords[1]) * NZ + coords[2]).astype(jnp.int32)
    snapshots = []
    for moment in range(NSTEPS):
        across, vertical = laplacians(current[0], current[1])
        source = jnp.zeros((NX * NY * NZ,), jnp.float32).at[flat_index].add(strengths[moment]).reshape(NX, NY, NZ)
        main_next = 2.0 * current[0] - previous[0] + coefs[0] * across + coefs[1] * vertical + source
        aux_next = 2.0 * current[1] - previous[1] + coefs[1] * across + coefs[2] * vertical + source
        previous = current
        current = jnp.stack([main_next, aux_next])
        if (moment + 1) % SNAP == 0:
            snapshots.append(current[0])
    return snapshots

def reference(checkpoint, courant, epsilon, delta, positions, amplitudes, offsets):
    coefs = jnp.stack([courant + 2.0 * courant * epsilon, courant * jnp.sqrt(2.0 * delta + 1.0), courant])
    zero_state = jnp.zeros_like(checkpoint[0, 0])
    pairs = []
    for shot in range(SHOTS):
        source_snaps = replay(checkpoint[shot, 0], checkpoint[shot, 1], coefs, positions[2 * shot], amplitudes[2 * shot])
        receiver_snaps = replay(zero_state, zero_state, coefs, positions[2 * shot + 1], amplitudes[2 * shot + 1])
        pairs.append((source_snaps, receiver_snaps))
    margins = ((HMAX, HMAX), (0, 0), (0, 0))

    def one_offset(shift):
        total = jnp.zeros((NX, NY, NZ), jnp.float32)
        for source_snaps, receiver_snaps in pairs:
            for number in range(len(source_snaps)):
                padded_source = jnp.pad(source_snaps[number], margins)
                shifted_source = lax.dynamic_slice_in_dim(padded_source, (HMAX - shift).astype(jnp.int32), NX, 0)
                padded_recv = jnp.pad(receiver_snaps[number], margins)
                shifted_recv = lax.dynamic_slice_in_dim(padded_recv, (HMAX + shift).astype(jnp.int32), NX, 0)
                total = total + shifted_source * shifted_recv
        return total
    return lax.map(one_offset, offsets)
```

```python
import functools
import jax
import jax.numpy as jnp
from jax import lax
from jax.experimental import pallas as pl
from jax.experimental.pallas import tpu as pltpu
from jax.sharding import PartitionSpec as P

SNAP = 4
HMAX = 8
PAIR = 2
ROWS = 8
LANES = 128
MESH = pl.DeviceIdType.MESH


def kernel(sizes, courant, epsilon, delta, checkpoint, positions, amplitudes, offsets, out,
           sg, sh, raw, cg, ch, pickg, pickh, spot, injg, injh, injb, ix, iy, idg, py, rx, ry, rd,
           snaps, fringe, outgoing, inbox,
           ls, isx, irx, isy, iry, isd, ird, hsx, hrx, hsy, hry, hsd, hrd, xs, xr, gs, gr):
    ng, nx, ny = sizes
    tx, ty, nz = courant.shape
    nrec = positions.shape[2]
    steps = amplitudes.shape[1]
    nh = offsets.shape[0]
    own = nh // ng
    turns = steps // PAIR
    blocks = steps // SNAP
    per = SNAP // PAIR
    d, a, b = lax.axis_index("grp"), lax.axis_index("gx"), lax.axis_index("gy")
    half = d % 2
    pair = d - half
    partner = {"grp": pair + 1 - half, "gx": a, "gy": b}
    edge = 1 if nx == 2 else 2
    width = tx + edge
    lead = a if nx == 2 else 1
    start = PAIR - lead
    right = PAIR + tx
    f32 = jnp.float32

    xside = (a > 0, a < nx - 1)
    yside = (b > 0, b < ny - 1)
    xdev = tuple({"grp": d, "gx": a + 2 * i - 1, "gy": b} for i in range(2))
    ydev = tuple({"grp": d, "gx": a, "gy": b + 2 * i - 1} for i in range(2))
    corners = [(i, j) for i in range(2) for j in range(2)]
    cthere = {(i, j): xside[i] & yside[j] for i, j in corners}
    cdev = {(i, j): {"grp": d, "gx": a + 2 * i - 1, "gy": b + 2 * j - 1} for i, j in corners}

    barrier = pltpu.get_barrier_semaphore()
    met = [(xside[i], xdev[i]) for i in range(2)] + [(yside[i], ydev[i]) for i in range(2)]
    met += [(cthere[c], cdev[c]) for c in corners]
    pl.semaphore_signal(barrier, inc=1, device_id=partner, device_id_type=MESH)
    for there, device in met:
        @pl.when(there)
        def _(device=device):
            pl.semaphore_signal(barrier, inc=1, device_id=device, device_id_type=MESH)

    models = (courant, epsilon, delta)

    def model_load(n):
        return pltpu.make_async_copy(models[n], raw.at[n], ls.at[n])

    def state_load(moment, field):
        return pltpu.make_async_copy(
            checkpoint.at[half, moment, field], sg.at[0, moment, field, pl.ds(PAIR, tx)], ls.at[3 + 2 * moment + field]
        )

    for n in range(3):
        model_load(n).start()

    for moment in range(2):
        for field in range(2):
            state_load(moment, field).start()

    big = jnp.zeros((ty, nz), f32)
    zero = jnp.zeros((ROWS, nz), f32)
    row = lax.broadcasted_iota(jnp.int32, (ROWS, nz), 0)
    lane = lax.broadcasted_iota(jnp.int32, (ROWS, LANES), 1)
    top, bottom, upper = row == 0, row == ROWS - 1, row < ROWS // 2

    def turn(v, shift, axis=0):
        shift = shift % v.shape[axis]
        return v if shift == 0 else pltpu.roll(v, shift, axis)

    for moment in range(2):
        for field in range(2):
            for x in range(tx + 2 * PAIR):
                sg[1, moment, field, x] = big
                for r in range(2):
                    sh[r, moment, field, x] = zero
            for x in (0, 1, right, right + 1):
                sg[0, moment, field, x] = big
    for n in range(3):
        for x in (0, 1, right, right + 1):
            cg[n, x] = big
            ch[n, x] = zero
    for side in range(2):
        @pl.when(jnp.logical_not(yside[side]))
        def _(side=side):
            for x in range(tx):
                iy[side, x] = zero
                for slot in range(2):
                    for r in range(2):
                        ry[slot, r, side, x] = zero
    for i, j in corners:
        @pl.when(jnp.logical_not(cthere[i, j]))
        def _(i=i, j=j):
            idg[i, j] = zero
            for slot in range(2):
                for r in range(2):
                    rd[slot, r, i, j] = zero

    total = 1
    for there, _ in met:
        total = total + there.astype(jnp.int32)
    pl.semaphore_wait(barrier, total)

    def first_x(side, n, arrival=False):
        last = tx - 1 if side else 0
        if n == 0:
            rows, target = pl.ds(tx - PAIR if side else 0, PAIR), pl.ds(0, PAIR)
        else:
            rows, target = pl.ds(last, 1), pl.ds(n + 1, 1)
        if n < 4:
            source = checkpoint.at[half, n // 2, n % 2, rows]
        else:
            source = models[n - 4].at[rows]
        into = side if arrival else 1 - side
        target = ix.at[into, target]
        return pltpu.make_async_remote_copy(
            src_ref=target if arrival else source, dst_ref=target, send_sem=isx.at[side, n],
            recv_sem=irx.at[into, n], device_id=xdev[side], device_id_type=MESH,
        )

    for side in range(2):
        @pl.when(xside[side])
        def _(side=side):
            for n in range(7):
                first_x(side, n).start()

    for n in range(3):
        model_load(n).wait()

    for moment in range(2):
        for field in range(2):
            state_load(moment, field).wait()

    def ends(v):
        return v[:ROWS], v[ty - ROWS:]

    for x in range(tx):
        tiles = [ends(sg[0, n // 2, n % 2, PAIR + x]) for n in range(4)]
        tiles += [ends(raw[n, x]) for n in range(3)]
        lower, higher = tiles[0]
        for n in range(1, 7):
            lower = jnp.where(row == n + 1, turn(tiles[n][0], n + 1), lower)
            higher = jnp.where(row == ROWS - 2 - n, turn(tiles[n][1], -n - 1), higher)
        py[0, 0, x] = lower
        py[0, 1, x] = higher

    def y_copy(r, target, send, recv, side, arrival=False):
        into = side if arrival else 1 - side
        return pltpu.make_async_remote_copy(
            src_ref=target.at[into] if arrival else py.at[r, side], dst_ref=target.at[into], send_sem=send.at[side],
            recv_sem=recv.at[into], device_id=ydev[side], device_id_type=MESH,
        )

    def d_copy(r, target, send, recv, corner, arrival=False):
        i, j = corner
        u, v = corner if arrival else (1 - i, 1 - j)
        return pltpu.make_async_remote_copy(
            src_ref=target.at[u, v] if arrival else py.at[r, j, tx - 1 if i else 0], dst_ref=target.at[u, v],
            send_sem=send.at[i, j], recv_sem=recv.at[u, v], device_id=cdev[corner], device_id_type=MESH,
        )

    for c in corners:
        @pl.when(cthere[c])
        def _(c=c):
            d_copy(0, idg, isd, ird, c).start()
    for side in range(2):
        @pl.when(yside[side])
        def _(side=side):
            y_copy(0, iy, isy, iry, side).start()

    def mix(c, e, v):
        return c + 2.0 * c * e, c * jnp.sqrt(2.0 * v + 1.0), c

    for x in range(tx):
        parts = mix(raw[0, x], raw[1, x], raw[2, x])
        for n in range(3):
            cg[n, PAIR + x] = parts[n]

    count = lax.broadcasted_iota(jnp.int32, (ty, nrec), 0)
    level = lax.broadcasted_iota(jnp.int32, (nz, nrec), 0)
    for r in range(2):
        line = pl.ds(2 * half + r, 1)
        px = positions[0, line, :] - (a * tx - lead)
        qy = positions[1, line, :] - b * ty
        pz = positions[2, line, :]
        column = (px >= 0) & (px < width)
        cell = jnp.where(column & (qy >= 0) & (qy < ty), px * ty + qy, -1)
        brim = jnp.where(column & (qy == ty), px * ROWS, jnp.where(column & (qy == -1), px * ROWS + ROWS - 1, -1))
        for w in range(width):
            pickg[r, pl.ds(w * ty, ty), :] = jnp.where(count + w * ty == cell, 1.0, 0.0).astype(jnp.bfloat16)
        for w in range((width + 1) // 2):
            pickh[r, pl.ds(w * ty, ty), :] = jnp.where(count + w * ty == brim, 1.0, 0.0).astype(jnp.bfloat16)
        where_z = jnp.where(level == pz, 1.0, 0.0).T.astype(jnp.bfloat16)
        spot[r, pl.ds(0, nrec), :] = where_z
        spot[r, pl.ds(nrec, nrec), :] = where_z

    def blank(j, carry):
        for r in range(2):
            for x in range(HMAX):
                snaps[j, r, x] = big
                snaps[j, r, HMAX + tx + x] = big
        return carry

    lax.fori_loop(0, blocks, blank, 0)

    def inject(turn_index, r):
        def strength(moment):
            s = jnp.broadcast_to(amplitudes[2 * half + r, pl.ds(moment, 1), :], (ty, nrec))
            high = s.astype(jnp.bfloat16)
            low = (s - high.astype(f32)).astype(jnp.bfloat16)
            return high, low

        def weigh(ref, base, n, parts):
            p = ref[r, pl.ds(base + n * ty, ty), :]
            return jnp.concatenate([p * parts[0], p * parts[1]], axis=1)

        one, two = strength(PAIR * turn_index), strength(PAIR * turn_index + 1)
        ours = pl.multiple_of(lead * ty, ty) if nx == 2 else lead * ty
        rows = [weigh(pickg, 0, n, one) for n in range(width)]
        rows += [weigh(pickh, 0, n, one) for n in range((width + 1) // 2)]
        rows += [weigh(pickg, ours, n, two) for n in range(tx)]
        found = jnp.dot(jnp.concatenate(rows, axis=0), spot[r], preferred_element_type=f32)
        low, high = width * ty, (width + (width + 1) // 2) * ty
        injg[r] = found[:low]
        injh[r] = found[low:high]
        injb[r] = found[high:]

    def down(v):
        tiles = [v[:, n * LANES:(n + 1) * LANES] for n in range(nz // LANES)]
        fore = [turn(t, 1, 1) for t in tiles]
        back = [turn(t, -1, 1) for t in tiles]
        sums = []
        for n, t in enumerate(tiles):
            before = jnp.where(lane == 0, fore[n - 1] if n else 0.0, fore[n])
            after = jnp.where(lane == LANES - 1, back[n + 1] if n + 1 < len(tiles) else 0.0, back[n])
            sums.append(before + after - 2.0 * t)
        return jnp.concatenate(sums, axis=1)

    def tiles_of(r, now, field, slot, brim):
        v = sg[r, now, field, slot]
        parts = [v[n * ROWS:(n + 1) * ROWS] for n in range(ty // ROWS)]
        return parts + ([sh[r, now, field, slot]] if brim else [])

    def advance(r, now, base, span, brim, gref, href):
        then = 1 - now
        full = ty // ROWS
        size = full + (1 if brim else 0)
        behind, here = tiles_of(r, now, 0, base - 1, brim), tiles_of(r, now, 0, base, True)
        for w in range(span):
            slot = base + w
            ahead = tiles_of(r, now, 0, slot + 1, True)
            ups, downs = [turn(t, 1) for t in here], [turn(t, -1) for t in here]
            for n in range(size):
                north = jnp.where(top, ups[n - 1], ups[n])
                south = jnp.where(bottom, downs[(n + 1) % (full + 1)], downs[n])
                m = here[n]
                across = (north + south) + (behind[n] + ahead[n]) - 4.0 * m
                if n < full:
                    part = pl.ds(n * ROWS, ROWS)
                    cur = sg.at[r, now, 1, slot, part]
                    prev = (sg.at[r, then, 0, slot, part], sg.at[r, then, 1, slot, part])
                    hor, cpl, ver = (cg[k, slot, part] for k in range(3))
                    source = gref[r, pl.ds(w * ty + n * ROWS, ROWS), :]
                else:
                    cur, prev = sh.at[r, now, 1, slot], (sh.at[r, then, 0, slot], sh.at[r, then, 1, slot])
                    hor, cpl, ver = (ch[k, slot] for k in range(3))
                    source = href[r, pl.ds(w * ROWS, ROWS), :]
                aux = cur[...]
                vertical = down(aux)
                prev[0][...] = 2.0 * m - prev[0][...] + hor * across + cpl * vertical + source
                prev[1][...] = 2.0 * aux - prev[1][...] + cpl * across + ver * vertical + source
            behind, here = here, ahead

    def first_merge():
        for side in range(2):
            @pl.when(yside[side])
            def _(side=side):
                y_copy(0, iy, isy, iry, side, True).wait_recv()
                y_copy(0, iy, isy, iry, side).wait_send()
        for c in corners:
            @pl.when(cthere[c])
            def _(c=c):
                d_copy(0, idg, isd, ird, c, True).wait_recv()
                d_copy(0, idg, isd, ird, c).wait_send()
        for side in range(2):
            @pl.when(xside[side])
            def _(side=side):
                for n in range(7):
                    first_x(side, n, True).wait_recv()
                    first_x(side, n).wait_send()

        for x in range(tx):
            below, above = iy[0, x], iy[1, x]

            def field(n):
                if n == 0:
                    return jnp.where(upper, above, below)
                return jnp.where(upper, turn(above, -n - 1), turn(below, n + 1))

            for n in range(4):
                sh[0, n // 2, n % 2, PAIR + x] = field(n)
            parts = mix(*(jnp.where(top | bottom, field(4 + n), 0.0) for n in range(3)))
            for n in range(3):
                ch[n, PAIR + x] = parts[n]
        for side in range(2):
            @pl.when(xside[side])
            def _(side=side):
                near, low = (right, right) if side else (1, 0)
                for n in range(PAIR):
                    sg[0, 0, 0, low + n] = ix[side, n]
                for n in range(1, 4):
                    sg[0, n // 2, n % 2, near] = ix[side, n + 1]
                parts = mix(ix[side, 5], ix[side, 6], ix[side, 7])
                for n in range(3):
                    cg[n, near] = parts[n]
                sh[0, 0, 0, near] = jnp.where(upper, idg[side, 1], idg[side, 0])

    def x_copy(slot, r, side, n, arrival=False):
        if n == 0:
            rows, target = pl.ds(right - PAIR if side else PAIR, PAIR), pl.ds(0, PAIR)
        else:
            rows, target = pl.ds(right - 1 if side else PAIR, 1), pl.ds(PAIR, 1)
        into = side if arrival else 1 - side
        target = rx.at[slot, r, into, target]
        return pltpu.make_async_remote_copy(
            src_ref=target if arrival else sg.at[r, 0, n, rows], dst_ref=target, send_sem=hsx.at[slot, r, side, n],
            recv_sem=hrx.at[slot, r, into, n], device_id=xdev[side], device_id_type=MESH,
        )

    def halo_y(slot, r, side, arrival=False):
        return y_copy(r, ry.at[slot, r], hsy.at[slot, r], hry.at[slot, r], side, arrival)

    def halo_d(slot, r, corner, arrival=False):
        return d_copy(r, rd.at[slot, r], hsd.at[slot, r], hrd.at[slot, r], corner, arrival)

    def merge(slot, r):
        for side in range(2):
            @pl.when(yside[side])
            def _(side=side):
                halo_y(slot, r, side, True).wait_recv()
                halo_y(slot, r, side).wait_send()
        for x in range(tx):
            below, above = ry[slot, r, 0, x], ry[slot, r, 1, x]
            sh[r, 0, 0, PAIR + x] = jnp.where(upper, above, below)
            sh[r, 0, 1, PAIR + x] = jnp.where(upper, turn(above, -2), turn(below, 2))
        for c in corners:
            @pl.when(cthere[c])
            def _(c=c):
                halo_d(slot, r, c, True).wait_recv()
                halo_d(slot, r, c).wait_send()
        for side in range(2):
            @pl.when(xside[side])
            def _(side=side):
                for n in range(2):
                    x_copy(slot, r, side, n, True).wait_recv()
                    x_copy(slot, r, side, n).wait_send()
                near, low = (right, right) if side else (1, 0)
                for n in range(PAIR):
                    sg[r, 0, 0, low + n] = rx[slot, r, side, n]
                sg[r, 0, 1, near] = rx[slot, r, side, PAIR]
                sh[r, 0, 0, near] = jnp.where(upper, rd[slot, r, side, 1], rd[slot, r, side, 0])

    def send(slot, r):
        for side in range(2):
            @pl.when(xside[side])
            def _(side=side):
                for n in range(2):
                    x_copy(slot, r, side, n).start()
        for x in range(tx):
            m, w = ends(sg[r, 0, 0, PAIR + x]), ends(sg[r, 0, 1, PAIR + x])
            py[r, 0, x] = jnp.where(row == 2, turn(w[0], 2), m[0])
            py[r, 1, x] = jnp.where(row == ROWS - 3, turn(w[1], -2), m[1])
        for c in corners:
            @pl.when(cthere[c])
            def _(c=c):
                halo_d(slot, r, c).start()
        for side in range(2):
            @pl.when(yside[side])
            def _(side=side):
                halo_y(slot, r, side).start()

    def fringe_copy(j, r, side, arrival=False):
        into = side if arrival else 1 - side
        source = snaps.at[j, r, pl.ds(tx, HMAX) if side else pl.ds(HMAX, HMAX)]
        target = fringe.at[j, r, into]
        return pltpu.make_async_remote_copy(
            src_ref=target if arrival else source, dst_ref=target, send_sem=xs.at[j, r, side],
            recv_sem=xr.at[j, r, into], device_id=xdev[side], device_id_type=MESH,
        )

    def send_fringe(j, r):
        for side in range(2):
            @pl.when(xside[side])
            def _(side=side):
                fringe_copy(j, r, side).start()

    def merge_fringe(j, r):
        for side in range(2):
            @pl.when(xside[side])
            def _(side=side):
                fringe_copy(j, r, side, True).wait_recv()
                fringe_copy(j, r, side).wait_send()
                for x in range(HMAX):
                    snaps[j, r, side * (HMAX + tx) + x] = fringe[j, r, side, x]

    def cycle(e, carry):
        for r in range(2):
            inject(e, r)

        @pl.when(e == 0)
        def _():
            first_merge()

        for r in range(2):
            @pl.when(e > 0)
            def _(r=r):
                merge(e % 2, r)

            advance(r, 0, start, width, True, injg, injh)
            advance(r, 1, PAIR, tx, False, injb, None)

            @pl.when(e < turns - 1)
            def _(r=r):
                send((e + 1) % 2, r)

        @pl.when(e % per == per - 1)
        def _():
            j = e // per
            for r in range(2):
                for x in range(tx):
                    snaps[j, r, HMAX + x] = sg[r, 0, 0, PAIR + x]
            send_fringe(j, 0)

        @pl.when(e == turns - 1)
        def _():
            send_fringe(blocks - 1, 1)

        @pl.when((e % per == 0) & (e > 0))
        def _():
            send_fringe(e // per - 1, 1)

        return carry

    lax.fori_loop(0, turns, cycle, 0)

    def swap_copy(n, rows, part):
        return pltpu.make_async_remote_copy(
            src_ref=outgoing.at[n, rows], dst_ref=inbox.at[n, rows], send_sem=gs.at[part, n], recv_sem=gr.at[part, n],
            device_id=partner, device_id_type=MESH,
        )

    def product(shift, x):
        sums = None
        for j in range(blocks):
            term = snaps[j, 0, HMAX - shift + x] * snaps[j, 1, HMAX + shift + x]
            sums = term if sums is None else sums + term
        return sums

    mid = tx // 2
    spans = [pl.ds(a * mid, mid), pl.ds((1 - a) * mid, mid)] if nx == 2 else [pl.ds(0, mid), pl.ds(mid, mid)]

    def fringes():
        for r in range(2):
            def one(j, carry, r=r):
                merge_fringe(j, r)
                return carry

            lax.fori_loop(0, blocks, one, 0)

    if nx != 2:
        fringes()
    for part, rows in enumerate(spans):
        if nx == 2 and part == 1:
            fringes()

        def theirs(n, carry, part=part, rows=rows):
            shift = offsets[pair * own + (1 - half) * own + n]
            for x in range(mid):
                outgoing[n, rows.start + x] = product(shift, rows.start + x)
            swap_copy(n, rows, part).start()
            return carry

        def ours(n, carry, rows=rows):
            shift = offsets[pair * own + half * own + n]
            for x in range(mid):
                out[n, rows.start + x] = product(shift, rows.start + x)
            return carry

        lax.fori_loop(0, own, theirs, 0)
        lax.fori_loop(0, own, ours, 0)
    for part, rows in enumerate(spans):
        def done(n, carry, part=part, rows=rows):
            swap_copy(n, rows, part).wait_recv()
            swap_copy(n, rows, part).wait_send()
            for x in range(mid):
                out[n, rows.start + x] = out[n, rows.start + x] + inbox[n, rows.start + x]
            return carry

        lax.fori_loop(0, own, done, 0)


def shards(sizes, checkpoint, courant, epsilon, delta, positions, amplitudes, offsets):
    ng, nx, ny = sizes
    shots = checkpoint.shape[0]
    tx, ty, nz = courant.shape
    nrec = positions.shape[2]
    steps = amplitudes.shape[1]
    blocks = steps // SNAP
    nh = offsets.shape[0]
    own = nh // ng
    assert ng == 2 * shots == 4 and ty == 2 * ROWS and tx >= HMAX and nz % LANES == 0 and nh % ng == 0 and nx > 1
    width = tx + (1 if nx == 2 else 2)
    wide = (width + 1) // 2
    slots = tx + 2 * PAIR
    f32, bf16 = jnp.float32, jnp.bfloat16
    dma = pltpu.SemaphoreType.DMA
    vmem = pl.BlockSpec(memory_space=pltpu.VMEM)
    anywhere = pl.BlockSpec(memory_space=pl.ANY)
    return pl.pallas_call(
        functools.partial(kernel, sizes),
        out_shape=jax.ShapeDtypeStruct((own, tx, ty, nz), f32),
        in_specs=[anywhere] * 4 + [vmem] * 2 + [pl.BlockSpec(memory_space=pltpu.SMEM)],
        out_specs=vmem,
        scratch_shapes=[
            pltpu.VMEM((2, 2, 2, slots, ty, nz), f32),
            pltpu.VMEM((2, 2, 2, slots, ROWS, nz), f32),
            pltpu.VMEM((3, tx, ty, nz), f32),
            pltpu.VMEM((3, slots, ty, nz), f32),
            pltpu.VMEM((3, slots, ROWS, nz), f32),
            pltpu.VMEM((2, width * ty, nrec), bf16),
            pltpu.VMEM((2, wide * ty, nrec), bf16),
            pltpu.VMEM((2, 2 * nrec, nz), bf16),
            pltpu.VMEM((2, width * ty, nz), f32),
            pltpu.VMEM((2, wide * ty, nz), f32),
            pltpu.VMEM((2, tx * ty, nz), f32),
            pltpu.VMEM((2, 8, ty, nz), f32),
            pltpu.VMEM((2, tx, ROWS, nz), f32),
            pltpu.VMEM((2, 2, ROWS, nz), f32),
            pltpu.VMEM((2, 2, tx, ROWS, nz), f32),
            pltpu.VMEM((2, 2, 2, PAIR + 1, ty, nz), f32),
            pltpu.VMEM((2, 2, 2, tx, ROWS, nz), f32),
            pltpu.VMEM((2, 2, 2, 2, ROWS, nz), f32),
            pltpu.VMEM((blocks, 2, tx + 2 * HMAX, ty, nz), f32),
            pltpu.VMEM((blocks, 2, 2, HMAX, ty, nz), f32),
            pltpu.VMEM((own, tx, ty, nz), f32),
            pltpu.VMEM((own, tx, ty, nz), f32),
            dma((7,)),
            dma((2, 7)),
            dma((2, 7)),
            dma((2,)),
            dma((2,)),
            dma((2, 2)),
            dma((2, 2)),
            dma((2, 2, 2, 2)),
            dma((2, 2, 2, 2)),
            dma((2, 2, 2)),
            dma((2, 2, 2)),
            dma((2, 2, 2, 2)),
            dma((2, 2, 2, 2)),
            dma((blocks, 2, 2)),
            dma((blocks, 2, 2)),
            dma((2, own)),
            dma((2, own)),
        ],
        compiler_params=pltpu.CompilerParams(
            collective_id=0, has_side_effects=True, vmem_limit_bytes=32 * 1024 * 1024
        ),
    )(courant, epsilon, delta, checkpoint, positions.transpose(1, 0, 2), amplitudes, offsets)


def solution(mesh):
    sizes = tuple(mesh.shape[axis] for axis in ("grp", "gx", "gy"))
    return jax.shard_map(
        functools.partial(shards, sizes),
        mesh=mesh,
        in_specs=(
            P(None, None, None, "gx", "gy", None),
            P("gx", "gy", None),
            P("gx", "gy", None),
            P("gx", "gy", None),
            P(),
            P(),
            P(),
        ),
        out_specs=P("grp", "gx", "gy", None),
        check_vma=False,
    )
```

```python
import functools
import jax
import jax.numpy as jnp
from jax import lax
from jax.experimental import pallas as pl
from jax.experimental.pallas import tpu as pltpu
from jax.sharding import PartitionSpec as P

SNAP = 4
HMAX = 8
PAIR = 2
ROWS = 8
LANES = 128
MESH = pl.DeviceIdType.MESH


def kernel(sizes, courant, epsilon, delta, checkpoint, positions, amplitudes, offsets, out,
           sg, sh, raw, cg, ch, pickg, pickh, spot, injg, injh, injb, ix, iy, idg, py, rx, ry, rd,
           snaps, fringe, outgoing, inbox,
           ls, isx, irx, isy, iry, isd, ird, hsx, hrx, hsy, hry, hsd, hrd, xs, xr, gs, gr):
    ng, nx, ny = sizes
    tx, ty, nz = courant.shape
    nrec = positions.shape[2]
    steps = amplitudes.shape[1]
    nh = offsets.shape[0]
    own = nh // ng
    turns = steps // PAIR
    blocks = steps // SNAP
    per = SNAP // PAIR
    d, a, b = lax.axis_index("grp"), lax.axis_index("gx"), lax.axis_index("gy")
    half = d % 2
    pair = d - half
    partner = {"grp": pair + 1 - half, "gx": a, "gy": b}
    edge = 1 if nx == 2 else 2
    width = tx + edge
    lead = a if nx == 2 else 1
    start = PAIR - lead
    right = PAIR + tx
    f32 = jnp.float32

    xside = (a > 0, a < nx - 1)
    yside = (b > 0, b < ny - 1)
    xdev = tuple({"grp": d, "gx": a + 2 * i - 1, "gy": b} for i in range(2))
    ydev = tuple({"grp": d, "gx": a, "gy": b + 2 * i - 1} for i in range(2))
    corners = [(i, j) for i in range(2) for j in range(2)]
    cthere = {(i, j): xside[i] & yside[j] for i, j in corners}
    cdev = {(i, j): {"grp": d, "gx": a + 2 * i - 1, "gy": b + 2 * j - 1} for i, j in corners}

    barrier = pltpu.get_barrier_semaphore()
    met = [(xside[i], xdev[i]) for i in range(2)] + [(yside[i], ydev[i]) for i in range(2)]
    met += [(cthere[c], cdev[c]) for c in corners]
    pl.semaphore_signal(barrier, inc=1, device_id=partner, device_id_type=MESH)
    for there, device in met:
        @pl.when(there)
        def _(device=device):
            pl.semaphore_signal(barrier, inc=1, device_id=device, device_id_type=MESH)

    models = (courant, epsilon, delta)

    def model_load(n):
        return pltpu.make_async_copy(models[n], raw.at[n], ls.at[n])

    def state_load(moment, field):
        return pltpu.make_async_copy(
            checkpoint.at[half, moment, field], sg.at[0, moment, field, pl.ds(PAIR, tx)], ls.at[3 + 2 * moment + field]
        )

    for n in range(3):
        model_load(n).start()

    for moment in range(2):
        for field in range(2):
            state_load(moment, field).start()

    big = jnp.zeros((ty, nz), f32)
    zero = jnp.zeros((ROWS, nz), f32)
    row = lax.broadcasted_iota(jnp.int32, (ROWS, nz), 0)
    lane = lax.broadcasted_iota(jnp.int32, (ROWS, LANES), 1)
    top, bottom, upper = row == 0, row == ROWS - 1, row < ROWS // 2

    def turn(v, shift, axis=0):
        shift = shift % v.shape[axis]
        return v if shift == 0 else pltpu.roll(v, shift, axis)

    for moment in range(2):
        for field in range(2):
            for x in range(tx + 2 * PAIR):
                sg[1, moment, field, x] = big
                for r in range(2):
                    sh[r, moment, field, x] = zero
            for x in (0, 1, right, right + 1):
                sg[0, moment, field, x] = big
    for n in range(3):
        for x in (0, 1, right, right + 1):
            cg[n, x] = big
            ch[n, x] = zero
    for side in range(2):
        @pl.when(jnp.logical_not(yside[side]))
        def _(side=side):
            for x in range(tx):
                iy[side, x] = zero
                for slot in range(2):
                    for r in range(2):
                        ry[slot, r, side, x] = zero
    for i, j in corners:
        @pl.when(jnp.logical_not(cthere[i, j]))
        def _(i=i, j=j):
            idg[i, j] = zero
            for slot in range(2):
                for r in range(2):
                    rd[slot, r, i, j] = zero

    total = 1
    for there, _ in met:
        total = total + there.astype(jnp.int32)
    pl.semaphore_wait(barrier, total)

    def first_x(side, n, arrival=False):
        last = tx - 1 if side else 0
        if n == 0:
            rows, target = pl.ds(tx - PAIR if side else 0, PAIR), pl.ds(0, PAIR)
        else:
            rows, target = pl.ds(last, 1), pl.ds(n + 1, 1)
        if n < 4:
            source = checkpoint.at[half, n // 2, n % 2, rows]
        else:
            source = models[n - 4].at[rows]
        into = side if arrival else 1 - side
        target = ix.at[into, target]
        return pltpu.make_async_remote_copy(
            src_ref=target if arrival else source, dst_ref=target, send_sem=isx.at[side, n],
            recv_sem=irx.at[into, n], device_id=xdev[side], device_id_type=MESH,
        )

    for side in range(2):
        @pl.when(xside[side])
        def _(side=side):
            for n in range(7):
                first_x(side, n).start()

    for n in range(3):
        model_load(n).wait()

    for moment in range(2):
        for field in range(2):
            state_load(moment, field).wait()

    def ends(v):
        return v[:ROWS], v[ty - ROWS:]

    for x in range(tx):
        tiles = [ends(sg[0, n // 2, n % 2, PAIR + x]) for n in range(4)]
        tiles += [ends(raw[n, x]) for n in range(3)]
        lower, higher = tiles[0]
        for n in range(1, 7):
            lower = jnp.where(row == n + 1, turn(tiles[n][0], n + 1), lower)
            higher = jnp.where(row == ROWS - 2 - n, turn(tiles[n][1], -n - 1), higher)
        py[0, 0, x] = lower
        py[0, 1, x] = higher

    def y_copy(r, target, send, recv, side, arrival=False):
        into = side if arrival else 1 - side
        return pltpu.make_async_remote_copy(
            src_ref=target.at[into] if arrival else py.at[r, side], dst_ref=target.at[into], send_sem=send.at[side],
            recv_sem=recv.at[into], device_id=ydev[side], device_id_type=MESH,
        )

    def d_copy(r, target, send, recv, corner, arrival=False):
        i, j = corner
        u, v = corner if arrival else (1 - i, 1 - j)
        return pltpu.make_async_remote_copy(
            src_ref=target.at[u, v] if arrival else py.at[r, j, tx - 1 if i else 0], dst_ref=target.at[u, v],
            send_sem=send.at[i, j], recv_sem=recv.at[u, v], device_id=cdev[corner], device_id_type=MESH,
        )

    for c in corners:
        @pl.when(cthere[c])
        def _(c=c):
            d_copy(0, idg, isd, ird, c).start()
    for side in range(2):
        @pl.when(yside[side])
        def _(side=side):
            y_copy(0, iy, isy, iry, side).start()

    def mix(c, e, v):
        return c + 2.0 * c * e, c * jnp.sqrt(2.0 * v + 1.0), c

    for x in range(tx):
        parts = mix(raw[0, x], raw[1, x], raw[2, x])
        for n in range(3):
            cg[n, PAIR + x] = parts[n]

    count = lax.broadcasted_iota(jnp.int32, (ty, nrec), 0)
    level = lax.broadcasted_iota(jnp.int32, (nz, nrec), 0)
    for r in range(2):
        line = pl.ds(2 * half + r, 1)
        px = positions[0, line, :] - (a * tx - lead)
        qy = positions[1, line, :] - b * ty
        pz = positions[2, line, :]
        column = (px >= 0) & (px < width)
        cell = jnp.where(column & (qy >= 0) & (qy < ty), px * ty + qy, -1)
        brim = jnp.where(column & (qy == ty), px * ROWS, jnp.where(column & (qy == -1), px * ROWS + ROWS - 1, -1))
        for w in range(width):
            pickg[r, pl.ds(w * ty, ty), :] = jnp.where(count + w * ty == cell, 1.0, 0.0).astype(jnp.bfloat16)
        for w in range((width + 1) // 2):
            pickh[r, pl.ds(w * ty, ty), :] = jnp.where(count + w * ty == brim, 1.0, 0.0).astype(jnp.bfloat16)
        where_z = jnp.where(level == pz, 1.0, 0.0).T.astype(jnp.bfloat16)
        spot[r, pl.ds(0, nrec), :] = where_z
        spot[r, pl.ds(nrec, nrec), :] = where_z

    def blank(j, carry):
        for r in range(2):
            for x in range(HMAX):
                snaps[j, r, x] = big
                snaps[j, r, HMAX + tx + x] = big
        return carry

    lax.fori_loop(0, blocks, blank, 0)

    def inject(turn_index, r):
        def strength(moment):
            s = jnp.broadcast_to(amplitudes[2 * half + r, pl.ds(moment, 1), :], (ty, nrec))
            high = s.astype(jnp.bfloat16)
            low = (s - high.astype(f32)).astype(jnp.bfloat16)
            return high, low

        def weigh(ref, base, n, parts):
            p = ref[r, pl.ds(base + n * ty, ty), :]
            return jnp.concatenate([p * parts[0], p * parts[1]], axis=1)

        one, two = strength(PAIR * turn_index), strength(PAIR * turn_index + 1)
        ours = pl.multiple_of(lead * ty, ty) if nx == 2 else lead * ty
        rows = [weigh(pickg, 0, n, one) for n in range(width)]
        rows += [weigh(pickh, 0, n, one) for n in range((width + 1) // 2)]
        rows += [weigh(pickg, ours, n, two) for n in range(tx)]
        found = jnp.dot(jnp.concatenate(rows, axis=0), spot[r], preferred_element_type=f32)
        low, high = width * ty, (width + (width + 1) // 2) * ty
        injg[r] = found[:low]
        injh[r] = found[low:high]
        injb[r] = found[high:]

    def down(v):
        tiles = [v[:, n * LANES:(n + 1) * LANES] for n in range(nz // LANES)]
        fore = [turn(t, 1, 1) for t in tiles]
        back = [turn(t, -1, 1) for t in tiles]
        sums = []
        for n, t in enumerate(tiles):
            before = jnp.where(lane == 0, fore[n - 1] if n else 0.0, fore[n])
            after = jnp.where(lane == LANES - 1, back[n + 1] if n + 1 < len(tiles) else 0.0, back[n])
            sums.append(before + after - 2.0 * t)
        return jnp.concatenate(sums, axis=1)

    def tiles_of(r, now, field, slot, brim):
        v = sg[r, now, field, slot]
        parts = [v[n * ROWS:(n + 1) * ROWS] for n in range(ty // ROWS)]
        return parts + ([sh[r, now, field, slot]] if brim else [])

    def advance(r, now, base, span, brim, gref, href):
        then = 1 - now
        full = ty // ROWS
        size = full + (1 if brim else 0)
        behind, here = tiles_of(r, now, 0, base - 1, brim), tiles_of(r, now, 0, base, True)
        for w in range(span):
            slot = base + w
            ahead = tiles_of(r, now, 0, slot + 1, True)
            ups, downs = [turn(t, 1) for t in here], [turn(t, -1) for t in here]
            for n in range(size):
                north = jnp.where(top, ups[n - 1], ups[n])
                south = jnp.where(bottom, downs[(n + 1) % (full + 1)], downs[n])
                m = here[n]
                across = (north + south) + (behind[n] + ahead[n]) - 4.0 * m
                if n < full:
                    part = pl.ds(n * ROWS, ROWS)
                    cur = sg.at[r, now, 1, slot, part]
                    prev = (sg.at[r, then, 0, slot, part], sg.at[r, then, 1, slot, part])
                    hor, cpl, ver = (cg[k, slot, part] for k in range(3))
                    source = gref[r, pl.ds(w * ty + n * ROWS, ROWS), :]
                else:
                    cur, prev = sh.at[r, now, 1, slot], (sh.at[r, then, 0, slot], sh.at[r, then, 1, slot])
                    hor, cpl, ver = (ch[k, slot] for k in range(3))
                    source = href[r, pl.ds(w * ROWS, ROWS), :]
                aux = cur[...]
                vertical = down(aux)
                prev[0][...] = 2.0 * m - prev[0][...] + hor * across + cpl * vertical + source
                prev[1][...] = 2.0 * aux - prev[1][...] + cpl * across + ver * vertical + source
            behind, here = here, ahead

    def first_merge():
        for side in range(2):
            @pl.when(yside[side])
            def _(side=side):
                y_copy(0, iy, isy, iry, side, True).wait_recv()
                y_copy(0, iy, isy, iry, side).wait_send()
        for c in corners:
            @pl.when(cthere[c])
            def _(c=c):
                d_copy(0, idg, isd, ird, c, True).wait_recv()
                d_copy(0, idg, isd, ird, c).wait_send()
        for side in range(2):
            @pl.when(xside[side])
            def _(side=side):
                for n in range(7):
                    first_x(side, n, True).wait_recv()
                    first_x(side, n).wait_send()

        for x in range(tx):
            below, above = iy[0, x], iy[1, x]

            def field(n):
                if n == 0:
                    return jnp.where(upper, above, below)
                return jnp.where(upper, turn(above, -n - 1), turn(below, n + 1))

            for n in range(4):
                sh[0, n // 2, n % 2, PAIR + x] = field(n)
            parts = mix(*(jnp.where(top | bottom, field(4 + n), 0.0) for n in range(3)))
            for n in range(3):
                ch[n, PAIR + x] = parts[n]
        for side in range(2):
            @pl.when(xside[side])
            def _(side=side):
                near, low = (right, right) if side else (1, 0)
                for n in range(PAIR):
                    sg[0, 0, 0, low + n] = ix[side, n]
                for n in range(1, 4):
                    sg[0, n // 2, n % 2, near] = ix[side, n + 1]
                parts = mix(ix[side, 5], ix[side, 6], ix[side, 7])
                for n in range(3):
                    cg[n, near] = parts[n]
                sh[0, 0, 0, near] = jnp.where(upper, idg[side, 1], idg[side, 0])

    def x_copy(slot, r, side, n, arrival=False):
        if n == 0:
            rows, target = pl.ds(right - PAIR if side else PAIR, PAIR), pl.ds(0, PAIR)
        else:
            rows, target = pl.ds(right - 1 if side else PAIR, 1), pl.ds(PAIR, 1)
        into = side if arrival else 1 - side
        target = rx.at[slot, r, into, target]
        return pltpu.make_async_remote_copy(
            src_ref=target if arrival else sg.at[r, 0, n, rows], dst_ref=target, send_sem=hsx.at[slot, r, side, n],
            recv_sem=hrx.at[slot, r, into, n], device_id=xdev[side], device_id_type=MESH,
        )

    def halo_y(slot, r, side, arrival=False):
        return y_copy(r, ry.at[slot, r], hsy.at[slot, r], hry.at[slot, r], side, arrival)

    def halo_d(slot, r, corner, arrival=False):
        return d_copy(r, rd.at[slot, r], hsd.at[slot, r], hrd.at[slot, r], corner, arrival)

    def merge(slot, r):
        for side in range(2):
            @pl.when(yside[side])
            def _(side=side):
                halo_y(slot, r, side, True).wait_recv()
                halo_y(slot, r, side).wait_send()
        for x in range(tx):
            below, above = ry[slot, r, 0, x], ry[slot, r, 1, x]
            sh[r, 0, 0, PAIR + x] = jnp.where(upper, above, below)
            sh[r, 0, 1, PAIR + x] = jnp.where(upper, turn(above, -2), turn(below, 2))
        for c in corners:
            @pl.when(cthere[c])
            def _(c=c):
                halo_d(slot, r, c, True).wait_recv()
                halo_d(slot, r, c).wait_send()
        for side in range(2):
            @pl.when(xside[side])
            def _(side=side):
                for n in range(2):
                    x_copy(slot, r, side, n, True).wait_recv()
                    x_copy(slot, r, side, n).wait_send()
                near, low = (right, right) if side else (1, 0)
                for n in range(PAIR):
                    sg[r, 0, 0, low + n] = rx[slot, r, side, n]
                sg[r, 0, 1, near] = rx[slot, r, side, PAIR]
                sh[r, 0, 0, near] = jnp.where(upper, rd[slot, r, side, 1], rd[slot, r, side, 0])

    def send(slot, r):
        for side in range(2):
            @pl.when(xside[side])
            def _(side=side):
                for n in range(2):
                    x_copy(slot, r, side, n).start()
        for x in range(tx):
            m, w = ends(sg[r, 0, 0, PAIR + x]), ends(sg[r, 0, 1, PAIR + x])
            py[r, 0, x] = jnp.where(row == 2, turn(w[0], 2), m[0])
            py[r, 1, x] = jnp.where(row == ROWS - 3, turn(w[1], -2), m[1])
        for c in corners:
            @pl.when(cthere[c])
            def _(c=c):
                halo_d(slot, r, c).start()
        for side in range(2):
            @pl.when(yside[side])
            def _(side=side):
                halo_y(slot, r, side).start()

    def fringe_copy(j, r, side, arrival=False):
        into = side if arrival else 1 - side
        source = snaps.at[j, r, pl.ds(tx, HMAX) if side else pl.ds(HMAX, HMAX)]
        target = fringe.at[j, r, into]
        return pltpu.make_async_remote_copy(
            src_ref=target if arrival else source, dst_ref=target, send_sem=xs.at[j, r, side],
            recv_sem=xr.at[j, r, into], device_id=xdev[side], device_id_type=MESH,
        )

    def send_fringe(j, r):
        for side in range(2):
            @pl.when(xside[side])
            def _(side=side):
                fringe_copy(j, r, side).start()

    def merge_fringe(j, r):
        for side in range(2):
            @pl.when(xside[side])
            def _(side=side):
                fringe_copy(j, r, side, True).wait_recv()
                fringe_copy(j, r, side).wait_send()
                for x in range(HMAX):
                    snaps[j, r, side * (HMAX + tx) + x] = fringe[j, r, side, x]

    def cycle(e, carry):
        for r in range(2):
            inject(e, r)

        @pl.when(e == 0)
        def _():
            first_merge()

        for r in range(2):
            @pl.when(e > 0)
            def _(r=r):
                merge(e % 2, r)

            advance(r, 0, start, width, True, injg, injh)
            advance(r, 1, PAIR, tx, False, injb, None)

            @pl.when(e < turns - 1)
            def _(r=r):
                send((e + 1) % 2, r)

        @pl.when(e % per == per - 1)
        def _():
            j = e // per
            for r in range(2):
                for x in range(tx):
                    snaps[j, r, HMAX + x] = sg[r, 0, 0, PAIR + x]
            send_fringe(j, 0)

        @pl.when(e == turns - 1)
        def _():
            send_fringe(blocks - 1, 1)

        @pl.when((e % per == 0) & (e > 0))
        def _():
            send_fringe(e // per - 1, 1)

        return carry

    lax.fori_loop(0, turns, cycle, 0)

    def swap_copy(n, rows, part):
        return pltpu.make_async_remote_copy(
            src_ref=outgoing.at[n, rows], dst_ref=inbox.at[n, rows], send_sem=gs.at[part, n], recv_sem=gr.at[part, n],
            device_id=partner, device_id_type=MESH,
        )

    def product(shift, x):
        sums = None
        for j in range(blocks):
            term = snaps[j, 0, HMAX - shift + x] * snaps[j, 1, HMAX + shift + x]
            sums = term if sums is None else sums + term
        return sums

    mid = tx // 2
    spans = [pl.ds(a * mid, mid), pl.ds((1 - a) * mid, mid)] if nx == 2 else [pl.ds(0, mid), pl.ds(mid, mid)]

    def fringes():
        for r in range(2):
            def one(j, carry, r=r):
                merge_fringe(j, r)
                return carry

            lax.fori_loop(0, blocks, one, 0)

    if nx != 2:
        fringes()
    for part, rows in enumerate(spans):
        if nx == 2 and part == 1:
            fringes()

        def theirs(n, carry, part=part, rows=rows):
            shift = offsets[pair * own + (1 - half) * own + n]
            for x in range(mid):
                outgoing[n, rows.start + x] = product(shift, rows.start + x)
            swap_copy(n, rows, part).start()
            return carry

        def ours(n, carry, rows=rows):
            shift = offsets[pair * own + half * own + n]
            for x in range(mid):
                out[n, rows.start + x] = product(shift, rows.start + x)
            return carry

        lax.fori_loop(0, own, theirs, 0)
        lax.fori_loop(0, own, ours, 0)
    for part, rows in enumerate(spans):
        def done(n, carry, part=part, rows=rows):
            swap_copy(n, rows, part).wait_recv()
            swap_copy(n, rows, part).wait_send()
            for x in range(mid):
                out[n, rows.start + x] = out[n, rows.start + x] + inbox[n, rows.start + x]
            return carry

        lax.fori_loop(0, own, done, 0)


def shards(sizes, checkpoint, courant, epsilon, delta, positions, amplitudes, offsets):
    ng, nx, ny = sizes
    shots = checkpoint.shape[0]
    tx, ty, nz = courant.shape
    nrec = positions.shape[2]
    steps = amplitudes.shape[1]
    blocks = steps // SNAP
    nh = offsets.shape[0]
    own = nh // ng
    assert ng == 2 * shots == 4 and ty == 2 * ROWS and tx >= HMAX and nz % LANES == 0 and nh % ng == 0 and nx > 1
    width = tx + (1 if nx == 2 else 2)
    wide = (width + 1) // 2
    slots = tx + 2 * PAIR
    f32, bf16 = jnp.float32, jnp.bfloat16
    dma = pltpu.SemaphoreType.DMA
    vmem = pl.BlockSpec(memory_space=pltpu.VMEM)
    anywhere = pl.BlockSpec(memory_space=pl.ANY)
    return pl.pallas_call(
        functools.partial(kernel, sizes),
        out_shape=jax.ShapeDtypeStruct((own, tx, ty, nz), f32),
        in_specs=[anywhere] * 4 + [vmem] * 2 + [pl.BlockSpec(memory_space=pltpu.SMEM)],
        out_specs=vmem,
        scratch_shapes=[
            pltpu.VMEM((2, 2, 2, slots, ty, nz), f32),
            pltpu.VMEM((2, 2, 2, slots, ROWS, nz), f32),
            pltpu.VMEM((3, tx, ty, nz), f32),
            pltpu.VMEM((3, slots, ty, nz), f32),
            pltpu.VMEM((3, slots, ROWS, nz), f32),
            pltpu.VMEM((2, width * ty, nrec), bf16),
            pltpu.VMEM((2, wide * ty, nrec), bf16),
            pltpu.VMEM((2, 2 * nrec, nz), bf16),
            pltpu.VMEM((2, width * ty, nz), f32),
            pltpu.VMEM((2, wide * ty, nz), f32),
            pltpu.VMEM((2, tx * ty, nz), f32),
            pltpu.VMEM((2, 8, ty, nz), f32),
            pltpu.VMEM((2, tx, ROWS, nz), f32),
            pltpu.VMEM((2, 2, ROWS, nz), f32),
            pltpu.VMEM((2, 2, tx, ROWS, nz), f32),
            pltpu.VMEM((2, 2, 2, PAIR + 1, ty, nz), f32),
            pltpu.VMEM((2, 2, 2, tx, ROWS, nz), f32),
            pltpu.VMEM((2, 2, 2, 2, ROWS, nz), f32),
            pltpu.VMEM((blocks, 2, tx + 2 * HMAX, ty, nz), f32),
            pltpu.VMEM((blocks, 2, 2, HMAX, ty, nz), f32),
            pltpu.VMEM((own, tx, ty, nz), f32),
            pltpu.VMEM((own, tx, ty, nz), f32),
            dma((7,)),
            dma((2, 7)),
            dma((2, 7)),
            dma((2,)),
            dma((2,)),
            dma((2, 2)),
            dma((2, 2)),
            dma((2, 2, 2, 2)),
            dma((2, 2, 2, 2)),
            dma((2, 2, 2)),
            dma((2, 2, 2)),
            dma((2, 2, 2, 2)),
            dma((2, 2, 2, 2)),
            dma((blocks, 2, 2)),
            dma((blocks, 2, 2)),
            dma((2, own)),
            dma((2, own)),
        ],
        compiler_params=pltpu.CompilerParams(
            collective_id=0, has_side_effects=True, vmem_limit_bytes=58720256
        ),
    )(courant, epsilon, delta, checkpoint, positions.transpose(1, 0, 2), amplitudes, offsets)


def solution(mesh):
    sizes = tuple(mesh.shape[axis] for axis in ("grp", "gx", "gy"))
    return jax.shard_map(
        functools.partial(shards, sizes),
        mesh=mesh,
        in_specs=(
            P(None, None, None, "gx", "gy", None),
            P("gx", "gy", None),
            P("gx", "gy", None),
            P("gx", "gy", None),
            P(),
            P(),
            P(),
        ),
        out_specs=P("grp", "gx", "gy", None),
        check_vma=False,
    )
```

```python
import functools
import jax
import jax.numpy as jnp
from jax import lax
from jax.experimental import pallas as pl
from jax.experimental.pallas import tpu as pltpu
from jax.sharding import PartitionSpec as P

SNAP = 4
HMAX = 8
PAIR = 2
ROWS = 8
LANES = 128
MESH = pl.DeviceIdType.MESH


def kernel(sizes, courant, epsilon, delta, checkpoint, positions, amplitudes, offsets, out,
           sg, sh, raw, cg, ch, pickg, pickh, pickb, spot, injg, injh, injb, ix, ixc, iy, idg, pi, py, pc, rx, ry, rd,
           snaps, fringe, outgoing,
           ls, isx, irx, isy, iry, isd, ird, hsx, hrx, hsy, hry, hsd, hrd, xs, xr, gs, gr):
    ng, nx, ny = sizes
    shots = checkpoint.shape[0]
    waves = 2 * shots
    tx, ty, nz = courant.shape
    nrec = positions.shape[2]
    steps = amplitudes.shape[1]
    own = offsets.shape[0] // ng
    turns = steps // PAIR
    blocks = steps // SNAP
    per = SNAP // PAIR
    d, a, b = lax.axis_index("grp"), lax.axis_index("gx"), lax.axis_index("gy")
    half = d % 2
    pair = d - half
    other = pair + 1 - half
    flip = b % 2
    hp = half + flip - 2 * half * flip
    partner = {"grp": other, "gx": a, "gy": b}
    width = tx + (1 if nx == 2 else 2)
    lead = a if nx == 2 else 1
    start = PAIR - lead
    right = PAIR + tx
    f32, bf16 = jnp.float32, jnp.bfloat16
    mine = pl.ds(pl.multiple_of(hp * ROWS, ROWS), ROWS)

    inner = (hp, 1 - hp)
    xside = (a > 0, a < nx - 1)
    yside = ((hp == 1) | (b > 0), (hp == 0) | (b < ny - 1))
    near_y = tuple((d + inner[i] * (other - d), b + (2 * i - 1) * (1 - inner[i])) for i in range(2))
    xdev = tuple({"grp": d, "gx": a + 2 * i - 1, "gy": b} for i in range(2))
    ydev = tuple({"grp": near_y[i][0], "gx": a, "gy": near_y[i][1]} for i in range(2))
    corners = [(i, j) for i in range(2) for j in range(2)]
    cthere = {(i, j): xside[i] & yside[j] for i, j in corners}
    cdev = {(i, j): {"grp": near_y[j][0], "gx": a + 2 * i - 1, "gy": near_y[j][1]} for i, j in corners}

    barrier = pltpu.get_barrier_semaphore()
    met = [(xside[i], xdev[i]) for i in range(2)] + [(yside[i], ydev[i]) for i in range(2)]
    met += [(cthere[c], cdev[c]) for c in corners]
    pl.semaphore_signal(barrier, inc=1, device_id=partner, device_id_type=MESH)
    for there, device in met:
        @pl.when(there)
        def _(device=device):
            pl.semaphore_signal(barrier, inc=1, device_id=device, device_id_type=MESH)

    models = (courant, epsilon, delta)

    def model_load(n):
        return pltpu.make_async_copy(models[n].at[:, mine, :], raw.at[n], ls.at[n])

    def state_load(s, moment, field):
        return pltpu.make_async_copy(
            checkpoint.at[s, moment, field, :, mine, :], sg.at[2 * s, moment, field, pl.ds(PAIR, tx)],
            ls.at[3 + 4 * s + 2 * moment + field],
        )

    loads = [(s, moment, field) for s in range(shots) for moment in range(2) for field in range(2)]
    for n in range(3):
        model_load(n).start()
    for load in loads:
        state_load(*load).start()

    zero = jnp.zeros((ROWS, nz), f32)
    row = lax.broadcasted_iota(jnp.int32, (ROWS, nz), 0)
    lane = lax.broadcasted_iota(jnp.int32, (ROWS, LANES), 1)
    top, bottom, upper = row == 0, row == ROWS - 1, row < ROWS // 2

    def turn(v, shift, axis=0):
        shift = shift % v.shape[axis]
        return v if shift == 0 else pltpu.roll(v, shift, axis)

    outer = (0, 1, right, right + 1)
    quad, mains = ROWS // PAIR, tx * PAIR // ROWS
    packs = mains + tx // ROWS

    def wipe(x, carry):
        for r in range(waves):
            for moment in range(2):
                for field in range(2):
                    if r % 2:
                        sg[r, moment, field, x] = zero
                    sh[r, moment, field, x] = zero
        return carry

    lax.fori_loop(0, tx + 2 * PAIR, wipe, 0)
    for x in outer:
        for s in range(shots):
            for moment in range(2):
                for field in range(2):
                    sg[2 * s, moment, field, x] = zero
        for n in range(3):
            cg[n, x] = zero
            ch[n, x] = zero
    for side in range(2):
        @pl.when(jnp.logical_not(yside[side]))
        def _(side=side):
            for x in range(tx):
                for s in range(shots):
                    iy[s, side, x] = zero
            for n in range(packs):
                for slot in range(2):
                    for r in range(waves):
                        ry[slot, r, side, n] = zero
    for i, j in corners:
        @pl.when(jnp.logical_not(cthere[i, j]))
        def _(i=i, j=j):
            for s in range(shots):
                idg[s, i, j] = zero
            for slot in range(2):
                for r in range(waves):
                    rd[slot, r, i, j] = zero[:1]

    total = 1
    for there, _ in met:
        total = total + there.astype(jnp.int32)
    pl.semaphore_wait(barrier, total)

    def first_x(side, s, n, arrival=False):
        last = pl.ds(tx - 1 if side else 0, 1)
        into = side if arrival else 1 - side
        if s < shots:
            rows = pl.ds(tx - PAIR if side else 0, PAIR) if n == 0 else last
            source = checkpoint.at[s, n // 2, n % 2, rows, mine, :]
            target = ix.at[into, s, pl.ds(0, PAIR) if n == 0 else pl.ds(n + 1, 1)]
        else:
            source, target = models[n].at[last, mine, :], ixc.at[into, pl.ds(n, 1)]
        return pltpu.make_async_remote_copy(
            src_ref=target if arrival else source, dst_ref=target, send_sem=isx.at[side, s, n],
            recv_sem=irx.at[into, s, n], device_id=xdev[side], device_id_type=MESH,
        )

    firsts = [(shots, n) for n in range(3)] + [(s, n) for s in range(shots) for n in range(4)]
    for side in range(2):
        @pl.when(xside[side])
        def _(side=side):
            for s, n in firsts:
                first_x(side, s, n).start()

    for n in range(3):
        model_load(n).wait()
    for load in loads:
        state_load(*load).wait()

    def first_y(s, side, arrival=False):
        into = side if arrival else 1 - side
        return pltpu.make_async_remote_copy(
            src_ref=iy.at[s, into] if arrival else pi.at[s, side], dst_ref=iy.at[s, into], send_sem=isy.at[s, side],
            recv_sem=iry.at[s, into], device_id=ydev[side], device_id_type=MESH,
        )

    def first_d(s, corner, arrival=False):
        i, j = corner
        u, v = corner if arrival else (1 - i, 1 - j)
        return pltpu.make_async_remote_copy(
            src_ref=idg.at[s, u, v] if arrival else pi.at[s, j, tx - 1 if i else 0], dst_ref=idg.at[s, u, v],
            send_sem=isd.at[s, i, j], recv_sem=ird.at[s, u, v], device_id=cdev[corner], device_id_type=MESH,
        )

    for s in range(shots):
        for x in range(tx):
            tiles = [sg[2 * s, n // 2, n % 2, PAIR + x] for n in range(4)]
            tiles += [raw[n, x] for n in range(3)] if s == 0 else []
            lower = higher = tiles[0]
            for n in range(1, len(tiles)):
                lower = jnp.where(row == n + 1, turn(tiles[n], n + 1), lower)
                higher = jnp.where(row == ROWS - 2 - n, turn(tiles[n], -n - 1), higher)
            pi[s, 0, x] = lower
            pi[s, 1, x] = higher
        for c in corners:
            @pl.when(cthere[c])
            def _(c=c, s=s):
                first_d(s, c).start()
        for side in range(2):
            @pl.when(yside[side])
            def _(side=side, s=s):
                first_y(s, side).start()

    def mix(c, e, v):
        return c + 2.0 * c * e, c * jnp.sqrt(2.0 * v + 1.0), c

    for x in range(tx):
        parts = mix(raw[0, x], raw[1, x], raw[2, x])
        for n in range(3):
            cg[n, PAIR + x] = parts[n]

    tile = 2 * ROWS
    wide = (width * ROWS + tile - 1) // tile
    count = lax.broadcasted_iota(jnp.int32, (tile, nrec), 0)
    level = lax.broadcasted_iota(jnp.int32, (nz, nrec), 0)
    for r in range(waves):
        px = positions[0, r:r + 1, :] - (a * tx - lead)
        qy = positions[1, r:r + 1, :] - (b * ty + hp * ROWS)
        pz = positions[2, r:r + 1, :]
        column = (px >= 0) & (px < width)
        within = (qy >= 0) & (qy < ROWS)
        cell = jnp.where(column & within, px * ROWS + qy, -1)
        brim = jnp.where(column & (qy == ROWS), px * ROWS, jnp.where(column & (qy == -1), px * ROWS + ROWS - 1, -1))
        core = jnp.where((px >= lead) & (px < lead + tx) & within, (px - lead) * ROWS + qy, -1)
        for ref, where, parts in ((pickg, cell, wide), (pickh, brim, wide), (pickb, core, tx * ROWS // tile)):
            for n in range(parts):
                ref[r, pl.ds(n * tile, tile), :] = jnp.where(count + n * tile == where, 1.0, 0.0).astype(bf16)
        where_z = jnp.where(level == pz, 1.0, 0.0).T.astype(bf16)
        spot[r, pl.ds(0, nrec), :] = where_z
        spot[r, pl.ds(nrec, nrec), :] = where_z

    def blank(j, carry):
        for r in range(waves):
            for x in range(HMAX):
                snaps[j, r, x] = zero
                snaps[j, r, HMAX + tx + x] = zero
        return carry

    lax.fori_loop(0, blocks, blank, 0)

    def inject(turn_index, r):
        def strength(moment):
            s = jnp.broadcast_to(amplitudes[r, pl.ds(moment, 1), :], (tile, nrec))
            high = s.astype(bf16)
            low = (s - high.astype(f32)).astype(bf16)
            return high, low

        def weigh(ref, n, parts):
            p = ref[r, pl.ds(n * tile, tile), :]
            return jnp.concatenate([p * parts[0], p * parts[1]], axis=1)

        one, two = strength(PAIR * turn_index), strength(PAIR * turn_index + 1)
        rows = [weigh(pickg, n, one) for n in range(wide)] + [weigh(pickh, n, one) for n in range(wide)]
        rows += [weigh(pickb, n, two) for n in range(tx * ROWS // tile)]
        found = jnp.dot(jnp.concatenate(rows, axis=0), spot[r], preferred_element_type=f32)
        injg[r] = found[:wide * tile]
        injh[r] = found[wide * tile:2 * wide * tile]
        injb[r] = found[2 * wide * tile:]

    def down(v):
        tiles = [v[:, n * LANES:(n + 1) * LANES] for n in range(nz // LANES)]
        fore = [turn(t, 1, 1) for t in tiles]
        back = [turn(t, -1, 1) for t in tiles]
        sums = []
        for n, t in enumerate(tiles):
            before = jnp.where(lane == 0, fore[n - 1] if n else 0.0, fore[n])
            after = jnp.where(lane == LANES - 1, back[n + 1] if n + 1 < len(tiles) else 0.0, back[n])
            sums.append(before + after - 2.0 * t)
        return jnp.concatenate(sums, axis=1)

    def advance(r, now, base, order, brim, gref, href):
        then = 1 - now

        def row_of(w, deep=True):
            slot = base + w
            return [sg[r, now, 0, slot]] + ([sh[r, now, 0, slot]] if deep else [])

        last = None
        for w in order:
            slot = base + w
            if last is not None and w == last + 1:
                behind, here = here, ahead
            else:
                behind, here = row_of(w - 1, brim), row_of(w)
            ahead = row_of(w + 1)
            last = w
            ups, downs = [turn(t, 1) for t in here], [turn(t, -1) for t in here]
            for n in range(2 if brim else 1):
                grid, coefs, source = (sh, ch, href) if n else (sg, cg, gref)
                north = jnp.where(top, ups[1 - n], ups[n])
                south = jnp.where(bottom, downs[1 - n], downs[n])
                m = here[n]
                across = (north + south) + (behind[n] + ahead[n]) - 4.0 * m
                aux = grid[r, now, 1, slot]
                vertical = down(aux)
                extra = source[r, pl.ds(w * ROWS, ROWS), :]
                hor, cpl, ver = (coefs[k, slot] for k in range(3))
                grid[r, then, 0, slot] = 2.0 * m - grid[r, then, 0, slot] + hor * across + cpl * vertical + extra
                grid[r, then, 1, slot] = 2.0 * aux - grid[r, then, 1, slot] + cpl * across + ver * vertical + extra

    def first_merge():
        for s in range(shots):
            for side in range(2):
                @pl.when(yside[side])
                def _(side=side, s=s):
                    first_y(s, side, True).wait_recv()
                    first_y(s, side).wait_send()
            for c in corners:
                @pl.when(cthere[c])
                def _(c=c, s=s):
                    first_d(s, c, True).wait_recv()
                    first_d(s, c).wait_send()
        for side in range(2):
            @pl.when(xside[side])
            def _(side=side):
                for s, n in firsts:
                    first_x(side, s, n, True).wait_recv()
                    first_x(side, s, n).wait_send()

        for s in range(shots):
            for x in range(tx):
                below, above = iy[s, 0, x], iy[s, 1, x]

                def field(n, below=below, above=above):
                    if n == 0:
                        return jnp.where(upper, above, below)
                    return jnp.where(upper, turn(above, -n - 1), turn(below, n + 1))

                for n in range(4):
                    sh[2 * s, n // 2, n % 2, PAIR + x] = field(n)
                if s == 0:
                    parts = mix(*(jnp.where(top | bottom, field(4 + n), 0.0) for n in range(3)))
                    for n in range(3):
                        ch[n, PAIR + x] = parts[n]
        for side in range(2):
            @pl.when(xside[side])
            def _(side=side):
                near, low = (right, right) if side else (1, 0)
                for s in range(shots):
                    for n in range(PAIR):
                        sg[2 * s, 0, 0, low + n] = ix[side, s, n]
                    for n in range(1, 4):
                        sg[2 * s, n // 2, n % 2, near] = ix[side, s, n + 1]
                    sh[2 * s, 0, 0, near] = jnp.where(upper, idg[s, side, 1], idg[s, side, 0])
                parts = mix(ixc[side, 0], ixc[side, 1], ixc[side, 2])
                for n in range(3):
                    cg[n, near] = parts[n]

    def halo_x(slot, r, side, n, arrival=False):
        if n == 0:
            rows, target = pl.ds(right - PAIR if side else PAIR, PAIR), pl.ds(0, PAIR)
        else:
            rows, target = pl.ds(right - 1 if side else PAIR, 1), pl.ds(PAIR, 1)
        into = side if arrival else 1 - side
        target = rx.at[slot, r, into, target]
        return pltpu.make_async_remote_copy(
            src_ref=target if arrival else sg.at[r, 0, n, rows], dst_ref=target, send_sem=hsx.at[slot, r, side, n],
            recv_sem=hrx.at[slot, r, into, n], device_id=xdev[side], device_id_type=MESH,
        )

    def halo_y(slot, r, side, arrival=False):
        into = side if arrival else 1 - side
        target = ry.at[slot, r, into]
        return pltpu.make_async_remote_copy(
            src_ref=target if arrival else py.at[r, side], dst_ref=target, send_sem=hsy.at[slot, r, side],
            recv_sem=hry.at[slot, r, into], device_id=ydev[side], device_id_type=MESH,
        )

    def halo_d(slot, r, corner, arrival=False):
        i, j = corner
        u, v = corner if arrival else (1 - i, 1 - j)
        target = rd.at[slot, r, u, v]
        return pltpu.make_async_remote_copy(
            src_ref=target if arrival else pc.at[r, i, j], dst_ref=target,
            send_sem=hsd.at[slot, r, i, j], recv_sem=hrd.at[slot, r, u, v], device_id=cdev[corner],
            device_id_type=MESH,
        )

    def corner(slot, r, side):
        above, below = (jnp.broadcast_to(rd[slot, r, side, n], (ROWS, nz)) for n in (1, 0))
        return jnp.where(upper, above, below)

    def merge(slot, r):
        for side in range(2):
            @pl.when(yside[side])
            def _(side=side):
                halo_y(slot, r, side, True).wait_recv()
                halo_y(slot, r, side).wait_send()
        for x in range(tx):
            n, k = x // quad, x % quad
            sh[r, 0, 0, PAIR + x] = jnp.where(
                upper, turn(ry[slot, r, 1, n], -PAIR * k), turn(ry[slot, r, 0, n], -PAIR * (k + 1))
            )
            n, k = mains + x // ROWS, x % ROWS
            sh[r, 0, 1, PAIR + x] = jnp.where(upper, turn(ry[slot, r, 1, n], -k), turn(ry[slot, r, 0, n], -k - 1))
        for c in corners:
            @pl.when(cthere[c])
            def _(c=c):
                halo_d(slot, r, c, True).wait_recv()
                halo_d(slot, r, c).wait_send()
        for side in range(2):
            @pl.when(xside[side])
            def _(side=side):
                for n in range(2):
                    halo_x(slot, r, side, n, True).wait_recv()
                    halo_x(slot, r, side, n).wait_send()
                near, low = (right, right) if side else (1, 0)
                for n in range(PAIR):
                    sg[r, 0, 0, low + n] = rx[slot, r, side, n]
                sg[r, 0, 1, near] = rx[slot, r, side, PAIR]
                sh[r, 0, 0, near] = corner(slot, r, side)

    def send_x(slot, r):
        for i, j in corners:
            v = sg[r, 0, 0, right - 1 if i else PAIR]
            pc[r, i, j] = v[ROWS - 1:] if j else v[:1]
        for c in corners:
            @pl.when(cthere[c])
            def _(c=c):
                halo_d(slot, r, c).start()
        for side in range(2):
            @pl.when(xside[side])
            def _(side=side):
                for n in range(2):
                    halo_x(slot, r, side, n).start()

    def send_y(slot, r):
        for n in range(packs):
            field, size, first = (0, PAIR, n * quad) if n < mains else (1, 1, (n - mains) * ROWS)
            lower = higher = None
            for k in range(ROWS // size):
                v = sg[r, 0, field, PAIR + first + k]
                one, two = turn(v, size * k), turn(v, size * (k + 1))
                lower = one if k == 0 else jnp.where(row < size * k, lower, one)
                higher = two if k == 0 else jnp.where(row < size * k, higher, two)
            py[r, 0, n] = lower
            py[r, 1, n] = higher
        for side in range(2):
            @pl.when(yside[side])
            def _(side=side):
                halo_y(slot, r, side).start()

    def fringe_copy(j, s, side, arrival=False):
        into = side if arrival else 1 - side
        both = pl.ds(2 * s, 2)
        target = fringe.at[j, into, both]
        return pltpu.make_async_remote_copy(
            src_ref=target if arrival else snaps.at[j, both, pl.ds(tx, HMAX) if side else pl.ds(HMAX, HMAX)],
            dst_ref=target, send_sem=xs.at[j, s, side], recv_sem=xr.at[j, s, into], device_id=xdev[side],
            device_id_type=MESH,
        )

    def send_fringe(j, s):
        for side in range(2):
            @pl.when(xside[side])
            def _(side=side):
                fringe_copy(j, s, side).start()

    def merge_fringe(j, carry):
        for s in range(shots):
            for side in range(2):
                @pl.when(xside[side])
                def _(side=side, s=s):
                    fringe_copy(j, s, side, True).wait_recv()
                    fringe_copy(j, s, side).wait_send()
                    for r in range(2 * s, 2 * s + 2):
                        for x in range(HMAX):
                            snaps[j, r, side * (HMAX + tx) + x] = fringe[j, side, r, x]
        return carry

    brink = list(range(PAIR)) + list(range(tx - PAIR, tx))
    rest = list(range(PAIR, tx - PAIR))

    def cycle(e, carry):
        for r in range(waves):
            inject(e, r)

        @pl.when(e == 0)
        def _():
            first_merge()

        for r in range(waves):
            @pl.when(e > 0)
            def _(r=r):
                merge(e % 2, r)

            advance(r, 0, start, range(width), True, injg, injh)
            advance(r, 1, PAIR, brink, False, injb, None)

            @pl.when(e < turns - 1)
            def _(r=r):
                send_x((e + 1) % 2, r)

            advance(r, 1, PAIR, rest, False, injb, None)

            @pl.when(e < turns - 1)
            def _(r=r):
                send_y((e + 1) % 2, r)

        @pl.when(e % per == per - 1)
        def _():
            j = e // per
            for r in range(waves):
                for x in range(tx):
                    snaps[j, r, HMAX + x] = sg[r, 0, 0, PAIR + x]
            send_fringe(j, 0)

        @pl.when(e == turns - 1)
        def _():
            for s in range(1, shots):
                send_fringe(blocks - 1, s)

        @pl.when((e % per == 0) & (e > 0))
        def _():
            for s in range(1, shots):
                send_fringe(e // per - 1, s)

        return carry

    lax.fori_loop(0, turns, cycle, 0)

    def swap_copy(n, rows, part):
        return pltpu.make_async_remote_copy(
            src_ref=outgoing.at[n, rows], dst_ref=out.at[n, rows, mine, :], send_sem=gs.at[part, n],
            recv_sem=gr.at[part, n], device_id=partner, device_id_type=MESH,
        )

    def product(shift, x):
        sums = None
        for j in range(blocks):
            for s in range(shots):
                term = snaps[j, 2 * s, HMAX - shift + x] * snaps[j, 2 * s + 1, HMAX + shift + x]
                sums = term if sums is None else sums + term
        return sums

    mid = tx // 2
    spans = [pl.ds(a * mid, mid), pl.ds((1 - a) * mid, mid)] if nx == 2 else [pl.ds(0, mid), pl.ds(mid, mid)]
    for part, rows in enumerate(spans):
        if part == (1 if nx == 2 else 0):
            lax.fori_loop(0, blocks, merge_fringe, 0)

        def theirs(n, carry, part=part, rows=rows):
            shift = offsets[pair * own + (1 - half) * own + n]
            for x in range(mid):
                outgoing[n, rows.start + x] = product(shift, rows.start + x)
            swap_copy(n, rows, part).start()
            return carry

        lax.fori_loop(0, own, theirs, 0)

    def ours(n, carry):
        shift = offsets[pair * own + half * own + n]
        for x in range(tx):
            out[n, x, mine, :] = product(shift, x)
        return carry

    lax.fori_loop(0, own, ours, 0)
    for part, rows in enumerate(spans):
        def done(n, carry, part=part, rows=rows):
            swap_copy(n, rows, part).wait_recv()
            swap_copy(n, rows, part).wait_send()
            return carry

        lax.fori_loop(0, own, done, 0)


def shards(sizes, checkpoint, courant, epsilon, delta, positions, amplitudes, offsets):
    ng, nx, ny = sizes
    shots = checkpoint.shape[0]
    waves = 2 * shots
    tx, ty, nz = courant.shape
    nrec = positions.shape[2]
    steps = amplitudes.shape[1]
    blocks = steps // SNAP
    nh = offsets.shape[0]
    own = nh // ng
    assert ng % 2 == 0 and ty == 2 * ROWS and tx == 2 * HMAX and nz % LANES == 0 and nh % ng == 0 and nx > 1
    assert shots <= 2 and steps % SNAP == 0
    width = tx + (1 if nx == 2 else 2)
    wide = (width + 1) // 2 * 2 * ROWS
    slots = tx + 2 * PAIR
    packs = tx * PAIR // ROWS + tx // ROWS
    f32, bf16 = jnp.float32, jnp.bfloat16
    dma = pltpu.SemaphoreType.DMA
    vmem = pl.BlockSpec(memory_space=pltpu.VMEM)
    anywhere = pl.BlockSpec(memory_space=pl.ANY)

    def held(*shape, dtype=f32):
        return pltpu.VMEM(shape, dtype)

    return pl.pallas_call(
        functools.partial(kernel, sizes),
        out_shape=jax.ShapeDtypeStruct((own, tx, ty, nz), f32),
        in_specs=[anywhere] * 4 + [vmem] * 2 + [pl.BlockSpec(memory_space=pltpu.SMEM)],
        out_specs=vmem,
        scratch_shapes=[
            held(waves, 2, 2, slots, ROWS, nz),
            held(waves, 2, 2, slots, ROWS, nz),
            held(3, tx, ROWS, nz),
            held(3, slots, ROWS, nz),
            held(3, slots, ROWS, nz),
            held(waves, wide, nrec, dtype=bf16),
            held(waves, wide, nrec, dtype=bf16),
            held(waves, tx * ROWS, nrec, dtype=bf16),
            held(waves, 2 * nrec, nz, dtype=bf16),
            held(waves, wide, nz),
            held(waves, wide, nz),
            held(waves, tx * ROWS, nz),
            held(2, shots, PAIR + 3, ROWS, nz),
            held(2, 3, ROWS, nz),
            held(shots, 2, tx, ROWS, nz),
            held(shots, 2, 2, ROWS, nz),
            held(shots, 2, tx, ROWS, nz),
            held(waves, 2, packs, ROWS, nz),
            held(waves, 2, 2, 1, nz),
            held(2, waves, 2, PAIR + 1, ROWS, nz),
            held(2, waves, 2, packs, ROWS, nz),
            held(2, waves, 2, 2, 1, nz),
            held(blocks, waves, tx + 2 * HMAX, ROWS, nz),
            held(blocks, 2, waves, HMAX, ROWS, nz),
            held(own, tx, ROWS, nz),
            dma((3 + 4 * shots,)),
            dma((2, shots + 1, 4)),
            dma((2, shots + 1, 4)),
            dma((shots, 2)),
            dma((shots, 2)),
            dma((shots, 2, 2)),
            dma((shots, 2, 2)),
            dma((2, waves, 2, 2)),
            dma((2, waves, 2, 2)),
            dma((2, waves, 2)),
            dma((2, waves, 2)),
            dma((2, waves, 2, 2)),
            dma((2, waves, 2, 2)),
            dma((blocks, shots, 2)),
            dma((blocks, shots, 2)),
            dma((2, own)),
            dma((2, own)),
        ],
        compiler_params=pltpu.CompilerParams(
            collective_id=0, has_side_effects=True, vmem_limit_bytes=58720256
        ),
    )(courant, epsilon, delta, checkpoint, positions.transpose(1, 0, 2), amplitudes, offsets)


def solution(mesh):
    sizes = tuple(mesh.shape[axis] for axis in ("grp", "gx", "gy"))
    return jax.shard_map(
        functools.partial(shards, sizes),
        mesh=mesh,
        in_specs=(
            P(None, None, None, "gx", "gy", None),
            P("gx", "gy", None),
            P("gx", "gy", None),
            P("gx", "gy", None),
            P(),
            P(),
            P(),
        ),
        out_specs=P("grp", "gx", "gy", None),
        check_vma=False,
    )
```

```python
import functools
import jax
import jax.numpy as jnp
from jax import lax
from jax.experimental import pallas as pl
from jax.experimental.pallas import tpu as pltpu
from jax.sharding import PartitionSpec as P

SNAP = 4
HMAX = 8
PAIR = 2
ROWS = 8
LANES = 128
MESH = pl.DeviceIdType.MESH


def kernel(sizes, courant, epsilon, delta, checkpoint, places, weights, shifts, out,
           positions, amplitudes, offsets, sg, sh, raw, cg, ch, pickg, pickh, pickb, spot, injg, injh, injb, ix, ixc, iy, idg, pi, py, pc, rx, ry, rd,
           snaps, fringe, outgoing,
           ls, isx, irx, isy, iry, isd, ird, hsx, hrx, hsy, hry, hsd, hrd, xs, xr, gs, gr):
    ng, nx, ny = sizes
    shots = checkpoint.shape[0]
    waves = 2 * shots
    tx, ty, nz = courant.shape
    nrec = positions.shape[2]
    steps = amplitudes.shape[1]
    own = offsets.shape[0] // ng
    turns = steps // PAIR
    blocks = steps // SNAP
    per = SNAP // PAIR
    d, a, b = lax.axis_index("grp"), lax.axis_index("gx"), lax.axis_index("gy")
    half = d % 2
    pair = d - half
    other = pair + 1 - half
    flip = b % 2
    hp = half + flip - 2 * half * flip
    partner = {"grp": other, "gx": a, "gy": b}
    width = tx + (1 if nx == 2 else 2)
    lead = a if nx == 2 else 1
    start = PAIR - lead
    right = PAIR + tx
    f32, bf16 = jnp.float32, jnp.bfloat16
    mine = pl.ds(pl.multiple_of(hp * ROWS, ROWS), ROWS)

    inner = (hp, 1 - hp)
    xside = (a > 0, a < nx - 1)
    yside = ((hp == 1) | (b > 0), (hp == 0) | (b < ny - 1))
    near_y = tuple((d + inner[i] * (other - d), b + (2 * i - 1) * (1 - inner[i])) for i in range(2))
    xdev = tuple({"grp": d, "gx": a + 2 * i - 1, "gy": b} for i in range(2))
    ydev = tuple({"grp": near_y[i][0], "gx": a, "gy": near_y[i][1]} for i in range(2))
    corners = [(i, j) for i in range(2) for j in range(2)]
    cthere = {(i, j): xside[i] & yside[j] for i, j in corners}
    cdev = {(i, j): {"grp": near_y[j][0], "gx": a + 2 * i - 1, "gy": near_y[j][1]} for i, j in corners}

    barrier = pltpu.get_barrier_semaphore()
    met = [(xside[i], xdev[i]) for i in range(2)] + [(yside[i], ydev[i]) for i in range(2)]
    met += [(cthere[c], cdev[c]) for c in corners]
    pl.semaphore_signal(barrier, inc=1, device_id=partner, device_id_type=MESH)
    for there, device in met:
        @pl.when(there)
        def _(device=device):
            pl.semaphore_signal(barrier, inc=1, device_id=device, device_id_type=MESH)

    models = (courant, epsilon, delta)

    def model_load(n):
        return pltpu.make_async_copy(models[n].at[:, mine, :], raw.at[n], ls.at[n])

    def state_load(s, moment, field):
        return pltpu.make_async_copy(
            checkpoint.at[s, moment, field, :, mine, :], sg.at[2 * s, moment, field, pl.ds(PAIR, tx)],
            ls.at[3 + 4 * s + 2 * moment + field],
        )

    loads = [(s, moment, field) for s in range(shots) for moment in range(2) for field in range(2)]
    tables = [
        pltpu.make_async_copy(source, target, ls.at[3 + 4 * shots + n])
        for n, (source, target) in enumerate(((places, positions), (weights, amplitudes), (shifts, offsets)))
    ]
    for n in range(3):
        model_load(n).start()
    for load in loads:
        state_load(*load).start()
    for table in tables:
        table.start()

    zero = jnp.zeros((ROWS, nz), f32)
    row = lax.broadcasted_iota(jnp.int32, (ROWS, nz), 0)
    lane = lax.broadcasted_iota(jnp.int32, (ROWS, LANES), 1)
    top, bottom, upper = row == 0, row == ROWS - 1, row < ROWS // 2

    def turn(v, shift, axis=0):
        shift = shift % v.shape[axis]
        return v if shift == 0 else pltpu.roll(v, shift, axis)

    outer = (0, 1, right, right + 1)
    quad, mains = ROWS // PAIR, tx * PAIR // ROWS
    packs = mains + tx // ROWS

    def wipe(x, carry):
        for r in range(waves):
            for moment in range(2):
                for field in range(2):
                    if r % 2:
                        sg[r, moment, field, x] = zero
                    sh[r, moment, field, x] = zero
        return carry

    lax.fori_loop(0, tx + 2 * PAIR, wipe, 0)
    for x in outer:
        for s in range(shots):
            for moment in range(2):
                for field in range(2):
                    sg[2 * s, moment, field, x] = zero
        for n in range(3):
            cg[n, x] = zero
            ch[n, x] = zero
    for side in range(2):
        @pl.when(jnp.logical_not(yside[side]))
        def _(side=side):
            for x in range(tx):
                for s in range(shots):
                    iy[s, side, x] = zero
            for n in range(packs):
                for slot in range(2):
                    for r in range(waves):
                        ry[slot, r, side, n] = zero
    for i, j in corners:
        @pl.when(jnp.logical_not(cthere[i, j]))
        def _(i=i, j=j):
            for s in range(shots):
                idg[s, i, j] = zero
            for slot in range(2):
                for r in range(waves):
                    rd[slot, r, i, j] = zero[:1]

    total = 1
    for there, _ in met:
        total = total + there.astype(jnp.int32)
    pl.semaphore_wait(barrier, total)

    def first_x(side, s, n, arrival=False):
        last = pl.ds(tx - 1 if side else 0, 1)
        into = side if arrival else 1 - side
        if s < shots:
            rows = pl.ds(tx - PAIR if side else 0, PAIR) if n == 0 else last
            source = checkpoint.at[s, n // 2, n % 2, rows, mine, :]
            target = ix.at[into, s, pl.ds(0, PAIR) if n == 0 else pl.ds(n + 1, 1)]
        else:
            source, target = models[n].at[last, mine, :], ixc.at[into, pl.ds(n, 1)]
        return pltpu.make_async_remote_copy(
            src_ref=target if arrival else source, dst_ref=target, send_sem=isx.at[side, s, n],
            recv_sem=irx.at[into, s, n], device_id=xdev[side], device_id_type=MESH,
        )

    firsts = [(shots, n) for n in range(3)] + [(s, n) for s in range(shots) for n in range(4)]
    for side in range(2):
        @pl.when(xside[side])
        def _(side=side):
            for s, n in firsts:
                first_x(side, s, n).start()

    for n in range(3):
        model_load(n).wait()
    for load in loads:
        state_load(*load).wait()

    def first_y(s, side, arrival=False):
        into = side if arrival else 1 - side
        return pltpu.make_async_remote_copy(
            src_ref=iy.at[s, into] if arrival else pi.at[s, side], dst_ref=iy.at[s, into], send_sem=isy.at[s, side],
            recv_sem=iry.at[s, into], device_id=ydev[side], device_id_type=MESH,
        )

    def first_d(s, corner, arrival=False):
        i, j = corner
        u, v = corner if arrival else (1 - i, 1 - j)
        return pltpu.make_async_remote_copy(
            src_ref=idg.at[s, u, v] if arrival else pi.at[s, j, tx - 1 if i else 0], dst_ref=idg.at[s, u, v],
            send_sem=isd.at[s, i, j], recv_sem=ird.at[s, u, v], device_id=cdev[corner], device_id_type=MESH,
        )

    for s in range(shots):
        for x in range(tx):
            tiles = [sg[2 * s, n // 2, n % 2, PAIR + x] for n in range(4)]
            tiles += [raw[n, x] for n in range(3)] if s == 0 else []
            lower = higher = tiles[0]
            for n in range(1, len(tiles)):
                lower = jnp.where(row == n + 1, turn(tiles[n], n + 1), lower)
                higher = jnp.where(row == ROWS - 2 - n, turn(tiles[n], -n - 1), higher)
            pi[s, 0, x] = lower
            pi[s, 1, x] = higher
        for c in corners:
            @pl.when(cthere[c])
            def _(c=c, s=s):
                first_d(s, c).start()
        for side in range(2):
            @pl.when(yside[side])
            def _(side=side, s=s):
                first_y(s, side).start()

    def mix(c, e, v):
        return c + 2.0 * c * e, c * jnp.sqrt(2.0 * v + 1.0), c

    for x in range(tx):
        parts = mix(raw[0, x], raw[1, x], raw[2, x])
        for n in range(3):
            cg[n, PAIR + x] = parts[n]

    for table in tables:
        table.wait()
    tile = 2 * ROWS
    wide = (width * ROWS + tile - 1) // tile
    count = lax.broadcasted_iota(jnp.int32, (tile, nrec), 0)
    level = lax.broadcasted_iota(jnp.int32, (nz, nrec), 0)
    for r in range(waves):
        px = positions[0, r:r + 1, :] - (a * tx - lead)
        qy = positions[1, r:r + 1, :] - (b * ty + hp * ROWS)
        pz = positions[2, r:r + 1, :]
        column = (px >= 0) & (px < width)
        within = (qy >= 0) & (qy < ROWS)
        cell = jnp.where(column & within, px * ROWS + qy, -1)
        brim = jnp.where(column & (qy == ROWS), px * ROWS, jnp.where(column & (qy == -1), px * ROWS + ROWS - 1, -1))
        core = jnp.where((px >= lead) & (px < lead + tx) & within, (px - lead) * ROWS + qy, -1)
        for ref, where, parts in ((pickg, cell, wide), (pickh, brim, wide), (pickb, core, tx * ROWS // tile)):
            for n in range(parts):
                ref[r, pl.ds(n * tile, tile), :] = jnp.where(count + n * tile == where, 1.0, 0.0).astype(bf16)
        where_z = jnp.where(level == pz, 1.0, 0.0).T.astype(bf16)
        spot[r, pl.ds(0, nrec), :] = where_z
        spot[r, pl.ds(nrec, nrec), :] = where_z

    def blank(j, carry):
        for r in range(waves):
            for x in range(HMAX):
                snaps[j, r, x] = zero
                snaps[j, r, HMAX + tx + x] = zero
        return carry

    lax.fori_loop(0, blocks, blank, 0)

    def inject(turn_index, r):
        def strength(moment):
            s = jnp.broadcast_to(amplitudes[r, pl.ds(moment, 1), :], (tile, nrec))
            high = s.astype(bf16)
            low = (s - high.astype(f32)).astype(bf16)
            return high, low

        def weigh(ref, n, parts):
            p = ref[r, pl.ds(n * tile, tile), :]
            return jnp.concatenate([p * parts[0], p * parts[1]], axis=1)

        one, two = strength(PAIR * turn_index), strength(PAIR * turn_index + 1)
        rows = [weigh(pickg, n, one) for n in range(wide)] + [weigh(pickh, n, one) for n in range(wide)]
        rows += [weigh(pickb, n, two) for n in range(tx * ROWS // tile)]
        found = jnp.dot(jnp.concatenate(rows, axis=0), spot[r], preferred_element_type=f32)
        injg[r] = found[:wide * tile]
        injh[r] = found[wide * tile:2 * wide * tile]
        injb[r] = found[2 * wide * tile:]

    def down(v):
        tiles = [v[:, n * LANES:(n + 1) * LANES] for n in range(nz // LANES)]
        fore = [turn(t, 1, 1) for t in tiles]
        back = [turn(t, -1, 1) for t in tiles]
        sums = []
        for n, t in enumerate(tiles):
            before = jnp.where(lane == 0, fore[n - 1] if n else 0.0, fore[n])
            after = jnp.where(lane == LANES - 1, back[n + 1] if n + 1 < len(tiles) else 0.0, back[n])
            sums.append(before + after - 2.0 * t)
        return jnp.concatenate(sums, axis=1)

    def advance(r, now, base, order, brim, gref, href):
        then = 1 - now

        def row_of(w, deep=True):
            slot = base + w
            return [sg[r, now, 0, slot]] + ([sh[r, now, 0, slot]] if deep else [])

        last = None
        for w in order:
            slot = base + w
            if last is not None and w == last + 1:
                behind, here = here, ahead
            else:
                behind, here = row_of(w - 1, brim), row_of(w)
            ahead = row_of(w + 1)
            last = w
            ups, downs = [turn(t, 1) for t in here], [turn(t, -1) for t in here]
            for n in range(2 if brim else 1):
                grid, coefs, source = (sh, ch, href) if n else (sg, cg, gref)
                north = jnp.where(top, ups[1 - n], ups[n])
                south = jnp.where(bottom, downs[1 - n], downs[n])
                m = here[n]
                across = (north + south) + (behind[n] + ahead[n]) - 4.0 * m
                aux = grid[r, now, 1, slot]
                vertical = down(aux)
                extra = source[r, pl.ds(w * ROWS, ROWS), :]
                hor, cpl, ver = (coefs[k, slot] for k in range(3))
                grid[r, then, 0, slot] = 2.0 * m - grid[r, then, 0, slot] + hor * across + cpl * vertical + extra
                grid[r, then, 1, slot] = 2.0 * aux - grid[r, then, 1, slot] + cpl * across + ver * vertical + extra

    def first_merge(s):
        for side in range(2):
            @pl.when(yside[side])
            def _(side=side):
                first_y(s, side, True).wait_recv()
                first_y(s, side).wait_send()
        for c in corners:
            @pl.when(cthere[c])
            def _(c=c):
                first_d(s, c, True).wait_recv()
                first_d(s, c).wait_send()

        for x in range(tx):
            below, above = iy[s, 0, x], iy[s, 1, x]

            def field(n, below=below, above=above):
                if n == 0:
                    return jnp.where(upper, above, below)
                return jnp.where(upper, turn(above, -n - 1), turn(below, n + 1))

            for n in range(4):
                sh[2 * s, n // 2, n % 2, PAIR + x] = field(n)
            if s == 0:
                parts = mix(*(jnp.where(top | bottom, field(4 + n), 0.0) for n in range(3)))
                for n in range(3):
                    ch[n, PAIR + x] = parts[n]
        for side in range(2):
            @pl.when(xside[side])
            def _(side=side):
                for group, n in firsts:
                    if group == s or (s == 0 and group == shots):
                        first_x(side, group, n, True).wait_recv()
                        first_x(side, group, n).wait_send()
                near, low = (right, right) if side else (1, 0)
                for n in range(PAIR):
                    sg[2 * s, 0, 0, low + n] = ix[side, s, n]
                for n in range(1, 4):
                    sg[2 * s, n // 2, n % 2, near] = ix[side, s, n + 1]
                sh[2 * s, 0, 0, near] = jnp.where(upper, idg[s, side, 1], idg[s, side, 0])
                if s == 0:
                    parts = mix(ixc[side, 0], ixc[side, 1], ixc[side, 2])
                    for n in range(3):
                        cg[n, near] = parts[n]

    def halo_x(slot, r, side, n, arrival=False):
        if n == 0:
            rows, target = pl.ds(right - PAIR if side else PAIR, PAIR), pl.ds(0, PAIR)
        else:
            rows, target = pl.ds(right - 1 if side else PAIR, 1), pl.ds(PAIR, 1)
        into = side if arrival else 1 - side
        target = rx.at[slot, r, into, target]
        return pltpu.make_async_remote_copy(
            src_ref=target if arrival else sg.at[r, 0, n, rows], dst_ref=target, send_sem=hsx.at[slot, r, side, n],
            recv_sem=hrx.at[slot, r, into, n], device_id=xdev[side], device_id_type=MESH,
        )

    def halo_y(slot, r, side, arrival=False):
        into = side if arrival else 1 - side
        target = ry.at[slot, r, into]
        return pltpu.make_async_remote_copy(
            src_ref=target if arrival else py.at[r, side], dst_ref=target, send_sem=hsy.at[slot, r, side],
            recv_sem=hry.at[slot, r, into], device_id=ydev[side], device_id_type=MESH,
        )

    def halo_d(slot, r, corner, arrival=False):
        i, j = corner
        u, v = corner if arrival else (1 - i, 1 - j)
        target = rd.at[slot, r, u, v]
        return pltpu.make_async_remote_copy(
            src_ref=target if arrival else pc.at[r, i, j], dst_ref=target,
            send_sem=hsd.at[slot, r, i, j], recv_sem=hrd.at[slot, r, u, v], device_id=cdev[corner],
            device_id_type=MESH,
        )

    def corner(slot, r, side):
        above, below = (jnp.broadcast_to(rd[slot, r, side, n], (ROWS, nz)) for n in (1, 0))
        return jnp.where(upper, above, below)

    def merge(slot, r):
        for side in range(2):
            @pl.when(yside[side])
            def _(side=side):
                halo_y(slot, r, side, True).wait_recv()
                halo_y(slot, r, side).wait_send()
        for x in range(tx):
            n, k = x // quad, x % quad
            sh[r, 0, 0, PAIR + x] = jnp.where(
                upper, turn(ry[slot, r, 1, n], -PAIR * k), turn(ry[slot, r, 0, n], -PAIR * (k + 1))
            )
            n, k = mains + x // ROWS, x % ROWS
            sh[r, 0, 1, PAIR + x] = jnp.where(upper, turn(ry[slot, r, 1, n], -k), turn(ry[slot, r, 0, n], -k - 1))
        for c in corners:
            @pl.when(cthere[c])
            def _(c=c):
                halo_d(slot, r, c, True).wait_recv()
                halo_d(slot, r, c).wait_send()
        for side in range(2):
            @pl.when(xside[side])
            def _(side=side):
                for n in range(2):
                    halo_x(slot, r, side, n, True).wait_recv()
                    halo_x(slot, r, side, n).wait_send()
                near, low = (right, right) if side else (1, 0)
                for n in range(PAIR):
                    sg[r, 0, 0, low + n] = rx[slot, r, side, n]
                sg[r, 0, 1, near] = rx[slot, r, side, PAIR]
                sh[r, 0, 0, near] = corner(slot, r, side)

    def send_x(slot, r):
        for i, j in corners:
            v = sg[r, 0, 0, right - 1 if i else PAIR]
            pc[r, i, j] = v[ROWS - 1:] if j else v[:1]
        for c in corners:
            @pl.when(cthere[c])
            def _(c=c):
                halo_d(slot, r, c).start()
        for side in range(2):
            @pl.when(xside[side])
            def _(side=side):
                for n in range(2):
                    halo_x(slot, r, side, n).start()

    def send_y(slot, r):
        for n in range(packs):
            field, size, first = (0, PAIR, n * quad) if n < mains else (1, 1, (n - mains) * ROWS)
            lower = higher = None
            for k in range(ROWS // size):
                v = sg[r, 0, field, PAIR + first + k]
                one, two = turn(v, size * k), turn(v, size * (k + 1))
                lower = one if k == 0 else jnp.where(row < size * k, lower, one)
                higher = two if k == 0 else jnp.where(row < size * k, higher, two)
            py[r, 0, n] = lower
            py[r, 1, n] = higher
        for side in range(2):
            @pl.when(yside[side])
            def _(side=side):
                halo_y(slot, r, side).start()

    def fringe_copy(j, s, side, arrival=False):
        into = side if arrival else 1 - side
        both = pl.ds(2 * s, 2)
        target = fringe.at[j, into, both]
        return pltpu.make_async_remote_copy(
            src_ref=target if arrival else snaps.at[j, both, pl.ds(tx, HMAX) if side else pl.ds(HMAX, HMAX)],
            dst_ref=target, send_sem=xs.at[j, s, side], recv_sem=xr.at[j, s, into], device_id=xdev[side],
            device_id_type=MESH,
        )

    def send_fringe(j, s):
        for side in range(2):
            @pl.when(xside[side])
            def _(side=side):
                fringe_copy(j, s, side).start()

    def merge_fringe(j, carry):
        for s in range(shots):
            for side in range(2):
                @pl.when(xside[side])
                def _(side=side, s=s):
                    fringe_copy(j, s, side, True).wait_recv()
                    fringe_copy(j, s, side).wait_send()
                    for r in range(2 * s, 2 * s + 2):
                        for x in range(HMAX):
                            snaps[j, r, side * (HMAX + tx) + x] = fringe[j, side, r, x]
        return carry

    brink = list(range(PAIR)) + list(range(tx - PAIR, tx))
    rest = list(range(PAIR, tx - PAIR))

    def cycle(e, carry):
        for r in range(waves):
            inject(e, r)

        for r in range(waves):
            if r % 2 == 0:
                @pl.when(e == 0)
                def _(r=r):
                    first_merge(r // 2)

            @pl.when(e > 0)
            def _(r=r):
                merge(e % 2, r)

            advance(r, 0, start, range(width), True, injg, injh)
            advance(r, 1, PAIR, brink, False, injb, None)

            @pl.when(e < turns - 1)
            def _(r=r):
                send_x((e + 1) % 2, r)

            advance(r, 1, PAIR, rest, False, injb, None)

            @pl.when(e < turns - 1)
            def _(r=r):
                send_y((e + 1) % 2, r)

            if r % 2 == 1:
                @pl.when(e % per == per - 1)
                def _(r=r):
                    for n in (r - 1, r):
                        for x in range(tx):
                            snaps[e // per, n, HMAX + x] = sg[n, 0, 0, PAIR + x]

                @pl.when(e == turns - 1)
                def _(r=r):
                    send_fringe(blocks - 1, r // 2)

        @pl.when((e % per == per - 1) & (e < turns - 1))
        def _():
            send_fringe(e // per, 0)

        @pl.when((e % per == 0) & (e > 0))
        def _():
            for s in range(1, shots):
                send_fringe(e // per - 1, s)

        return carry

    lax.fori_loop(0, turns, cycle, 0)

    def swap_copy(n, rows, part):
        return pltpu.make_async_remote_copy(
            src_ref=outgoing.at[n, rows], dst_ref=out.at[n, rows, mine, :], send_sem=gs.at[part, n],
            recv_sem=gr.at[part, n], device_id=partner, device_id_type=MESH,
        )

    def product(shift, x):
        sums = None
        for j in range(blocks):
            for s in range(shots):
                term = snaps[j, 2 * s, HMAX - shift + x] * snaps[j, 2 * s + 1, HMAX + shift + x]
                sums = term if sums is None else sums + term
        return sums

    mid = tx // 2
    spans = [pl.ds(a * mid, mid), pl.ds((1 - a) * mid, mid)] if nx == 2 else [pl.ds(0, mid), pl.ds(mid, mid)]
    for part, rows in enumerate(spans):
        if part == (1 if nx == 2 else 0):
            lax.fori_loop(0, blocks, merge_fringe, 0)

        def theirs(n, carry, part=part, rows=rows):
            shift = offsets[pair * own + (1 - half) * own + n]
            for x in range(mid):
                outgoing[n, rows.start + x] = product(shift, rows.start + x)
            swap_copy(n, rows, part).start()
            return carry

        lax.fori_loop(0, own, theirs, 0)

    def ours(n, carry):
        shift = offsets[pair * own + half * own + n]
        for x in range(tx):
            out[n, x, mine, :] = product(shift, x)
        return carry

    lax.fori_loop(0, own, ours, 0)
    for part, rows in enumerate(spans):
        def done(n, carry, part=part, rows=rows):
            swap_copy(n, rows, part).wait_recv()
            swap_copy(n, rows, part).wait_send()
            return carry

        lax.fori_loop(0, own, done, 0)


def shards(sizes, checkpoint, courant, epsilon, delta, positions, amplitudes, offsets):
    ng, nx, ny = sizes
    shots = checkpoint.shape[0]
    waves = 2 * shots
    tx, ty, nz = courant.shape
    nrec = positions.shape[2]
    steps = amplitudes.shape[1]
    blocks = steps // SNAP
    nh = offsets.shape[0]
    own = nh // ng
    assert ng % 2 == 0 and ty == 2 * ROWS and tx == 2 * HMAX and nz % LANES == 0 and nh % ng == 0 and nx > 1
    assert shots <= 2 and steps % SNAP == 0
    width = tx + (1 if nx == 2 else 2)
    wide = (width + 1) // 2 * 2 * ROWS
    slots = tx + 2 * PAIR
    packs = tx * PAIR // ROWS + tx // ROWS
    f32, bf16 = jnp.float32, jnp.bfloat16
    dma = pltpu.SemaphoreType.DMA
    vmem = pl.BlockSpec(memory_space=pltpu.VMEM)

    places = positions.transpose(1, 0, 2)
    arguments = (courant, epsilon, delta, checkpoint, places, amplitudes, offsets)

    def held(*shape, dtype=f32):
        return pltpu.VMEM(shape, dtype)

    return pl.pallas_call(
        functools.partial(kernel, sizes),
        out_shape=jax.ShapeDtypeStruct((own, tx, ty, nz), f32),
        in_specs=[pl.BlockSpec(memory_space=pltpu.HBM)] * 7,
        out_specs=vmem,
        scratch_shapes=[
            held(*places.shape, dtype=places.dtype),
            held(*amplitudes.shape),
            pltpu.SMEM(offsets.shape, offsets.dtype),
            held(waves, 2, 2, slots, ROWS, nz),
            held(waves, 2, 2, slots, ROWS, nz),
            held(3, tx, ROWS, nz),
            held(3, slots, ROWS, nz),
            held(3, slots, ROWS, nz),
            held(waves, wide, nrec, dtype=bf16),
            held(waves, wide, nrec, dtype=bf16),
            held(waves, tx * ROWS, nrec, dtype=bf16),
            held(waves, 2 * nrec, nz, dtype=bf16),
            held(waves, wide, nz),
            held(waves, wide, nz),
            held(waves, tx * ROWS, nz),
            held(2, shots, PAIR + 3, ROWS, nz),
            held(2, 3, ROWS, nz),
            held(shots, 2, tx, ROWS, nz),
            held(shots, 2, 2, ROWS, nz),
            held(shots, 2, tx, ROWS, nz),
            held(waves, 2, packs, ROWS, nz),
            held(waves, 2, 2, 1, nz),
            held(2, waves, 2, PAIR + 1, ROWS, nz),
            held(2, waves, 2, packs, ROWS, nz),
            held(2, waves, 2, 2, 1, nz),
            held(blocks, waves, tx + 2 * HMAX, ROWS, nz),
            held(blocks, 2, waves, HMAX, ROWS, nz),
            held(own, tx, ROWS, nz),
            dma((6 + 4 * shots,)),
            dma((2, shots + 1, 4)),
            dma((2, shots + 1, 4)),
            dma((shots, 2)),
            dma((shots, 2)),
            dma((shots, 2, 2)),
            dma((shots, 2, 2)),
            dma((2, waves, 2, 2)),
            dma((2, waves, 2, 2)),
            dma((2, waves, 2)),
            dma((2, waves, 2)),
            dma((2, waves, 2, 2)),
            dma((2, waves, 2, 2)),
            dma((blocks, shots, 2)),
            dma((blocks, shots, 2)),
            dma((2, own)),
            dma((2, own)),
        ],
        compiler_params=pltpu.CompilerParams(
            collective_id=0, has_side_effects=True, vmem_limit_bytes=44 * 1024 * 1024
        ),
    )(*(pltpu.with_memory_space_constraint(v, pltpu.HBM) for v in arguments))


def solution(mesh):
    sizes = tuple(mesh.shape[axis] for axis in ("grp", "gx", "gy"))
    return jax.shard_map(
        functools.partial(shards, sizes),
        mesh=mesh,
        in_specs=(
            P(None, None, None, "gx", "gy", None),
            P("gx", "gy", None),
            P("gx", "gy", None),
            P("gx", "gy", None),
            P(),
            P(),
            P(),
        ),
        out_specs=P("grp", "gx", "gy", None),
        check_vma=False,
    )
```

```python
import functools
import jax
import jax.numpy as jnp
from jax import lax
from jax.experimental import pallas as pl
from jax.experimental.pallas import tpu as pltpu
from jax.sharding import PartitionSpec as P

SNAP = 4
HMAX = 8
PAIR = 2
ROWS = 8
LANES = 128
MESH = pl.DeviceIdType.MESH


def kernel(sizes, courant, epsilon, delta, checkpoint, places, weights, shifts, out,
           positions, amplitudes, offsets, sg, sh, raw, cg, ch, pickg, pickh, pickb, spot, injg, injh, injb, ix, ixc, iy, idg, pi, py, pc, rx, ry, rd,
           snaps, fringe, outgoing,
           ls, isx, irx, isy, iry, isd, ird, hsx, hrx, hsy, hry, hsd, hrd, xs, xr, gs, gr):
    ng, nx, ny = sizes
    shots = checkpoint.shape[0]
    waves = 2 * shots
    tx, ty, nz = courant.shape
    nrec = positions.shape[2]
    steps = amplitudes.shape[1]
    own = offsets.shape[0] // ng
    turns = steps // PAIR
    blocks = steps // SNAP
    per = SNAP // PAIR
    d, a, b = lax.axis_index("grp"), lax.axis_index("gx"), lax.axis_index("gy")
    half = d % 2
    pair = d - half
    other = pair + 1 - half
    flip = b % 2
    hp = half + flip - 2 * half * flip
    partner = {"grp": other, "gx": a, "gy": b}
    width = tx + (1 if nx == 2 else 2)
    lead = a if nx == 2 else 1
    start = PAIR - lead
    right = PAIR + tx
    f32, bf16 = jnp.float32, jnp.bfloat16
    mine = pl.ds(pl.multiple_of(hp * ROWS, ROWS), ROWS)

    inner = (hp, 1 - hp)
    xside = (a > 0, a < nx - 1)
    yside = ((hp == 1) | (b > 0), (hp == 0) | (b < ny - 1))
    near_y = tuple((d + inner[i] * (other - d), b + (2 * i - 1) * (1 - inner[i])) for i in range(2))
    xdev = tuple({"grp": d, "gx": a + 2 * i - 1, "gy": b} for i in range(2))
    ydev = tuple({"grp": near_y[i][0], "gx": a, "gy": near_y[i][1]} for i in range(2))
    corners = [(i, j) for i in range(2) for j in range(2)]
    cthere = {(i, j): xside[i] & yside[j] for i, j in corners}
    cdev = {(i, j): {"grp": near_y[j][0], "gx": a + 2 * i - 1, "gy": near_y[j][1]} for i, j in corners}

    barrier = pltpu.get_barrier_semaphore()
    met = [(xside[i], xdev[i]) for i in range(2)] + [(yside[i], ydev[i]) for i in range(2)]
    met += [(cthere[c], cdev[c]) for c in corners]
    pl.semaphore_signal(barrier, inc=1, device_id=partner, device_id_type=MESH)
    for there, device in met:
        @pl.when(there)
        def _(device=device):
            pl.semaphore_signal(barrier, inc=1, device_id=device, device_id_type=MESH)

    models = (courant, epsilon, delta)

    def model_load(n):
        return pltpu.make_async_copy(models[n].at[:, mine, :], raw.at[n], ls.at[n])

    def state_load(s, moment, field):
        return pltpu.make_async_copy(
            checkpoint.at[s, moment, field, :, mine, :], sg.at[2 * s, moment, field, pl.ds(PAIR, tx)],
            ls.at[3 + 4 * s + 2 * moment + field],
        )

    loads = [(s, moment, field) for s in range(shots) for moment in range(2) for field in range(2)]
    tables = [
        pltpu.make_async_copy(source, target, ls.at[3 + 4 * shots + n])
        for n, (source, target) in enumerate(((places, positions), (weights, amplitudes), (shifts, offsets)))
    ]
    for n in range(3):
        model_load(n).start()
    for load in loads:
        state_load(*load).start()
    for table in tables:
        table.start()

    zero = jnp.zeros((ROWS, nz), f32)
    row = lax.broadcasted_iota(jnp.int32, (ROWS, nz), 0)
    lane = lax.broadcasted_iota(jnp.int32, (ROWS, LANES), 1)
    top, bottom, upper = row == 0, row == ROWS - 1, row < ROWS // 2

    def turn(v, shift, axis=0):
        shift = shift % v.shape[axis]
        return v if shift == 0 else pltpu.roll(v, shift, axis)

    outer = (0, 1, right, right + 1)
    quad, packs, strips = ROWS // PAIR, PAIR + 1, tx // ROWS

    def wipe(x, carry):
        for r in range(waves):
            for moment in range(2):
                for field in range(2):
                    if r % 2:
                        sg[r, moment, field, x] = zero
                    sh[r, moment, field, x] = zero
        return carry

    lax.fori_loop(0, tx + 2 * PAIR, wipe, 0)
    for x in outer:
        for s in range(shots):
            for moment in range(2):
                for field in range(2):
                    sg[2 * s, moment, field, x] = zero
        for n in range(3):
            cg[n, x] = zero
            ch[n, x] = zero
    for side in range(2):
        @pl.when(jnp.logical_not(yside[side]))
        def _(side=side):
            for x in range(tx):
                for s in range(shots):
                    iy[s, side, x] = zero
            for slot in range(2):
                for r in range(waves):
                    for strip in range(strips):
                        for n in range(packs):
                            ry[slot, r, side, strip, n] = zero
    for i, j in corners:
        @pl.when(jnp.logical_not(cthere[i, j]))
        def _(i=i, j=j):
            for s in range(shots):
                idg[s, i, j] = zero
            for slot in range(2):
                for r in range(waves):
                    rd[slot, r, i, j] = zero[:1]

    total = 1
    for there, _ in met:
        total = total + there.astype(jnp.int32)
    pl.semaphore_wait(barrier, total)

    def first_x(side, s, n, arrival=False):
        last = pl.ds(tx - 1 if side else 0, 1)
        into = side if arrival else 1 - side
        if s < shots:
            rows = pl.ds(tx - PAIR if side else 0, PAIR) if n == 0 else last
            source = checkpoint.at[s, n // 2, n % 2, rows, mine, :]
            target = ix.at[into, s, pl.ds(0, PAIR) if n == 0 else pl.ds(n + 1, 1)]
        else:
            source, target = models[n].at[last, mine, :], ixc.at[into, pl.ds(n, 1)]
        return pltpu.make_async_remote_copy(
            src_ref=target if arrival else source, dst_ref=target, send_sem=isx.at[side, s, n],
            recv_sem=irx.at[into, s, n], device_id=xdev[side], device_id_type=MESH,
        )

    firsts = [(shots, n) for n in range(3)] + [(s, n) for s in range(shots) for n in range(4)]
    for side in range(2):
        @pl.when(xside[side])
        def _(side=side):
            for s, n in firsts:
                first_x(side, s, n).start()

    for n in range(3):
        model_load(n).wait()
    for load in loads:
        state_load(*load).wait()

    def first_y(s, side, arrival=False):
        into = side if arrival else 1 - side
        return pltpu.make_async_remote_copy(
            src_ref=iy.at[s, into] if arrival else pi.at[s, side], dst_ref=iy.at[s, into], send_sem=isy.at[s, side],
            recv_sem=iry.at[s, into], device_id=ydev[side], device_id_type=MESH,
        )

    def first_d(s, corner, arrival=False):
        i, j = corner
        u, v = corner if arrival else (1 - i, 1 - j)
        return pltpu.make_async_remote_copy(
            src_ref=idg.at[s, u, v] if arrival else pi.at[s, j, tx - 1 if i else 0], dst_ref=idg.at[s, u, v],
            send_sem=isd.at[s, i, j], recv_sem=ird.at[s, u, v], device_id=cdev[corner], device_id_type=MESH,
        )

    for s in range(shots):
        for x in range(tx):
            tiles = [sg[2 * s, n // 2, n % 2, PAIR + x] for n in range(4)]
            tiles += [raw[n, x] for n in range(3)] if s == 0 else []
            lower = higher = tiles[0]
            for n in range(1, len(tiles)):
                lower = jnp.where(row == n + 1, turn(tiles[n], n + 1), lower)
                higher = jnp.where(row == ROWS - 2 - n, turn(tiles[n], -n - 1), higher)
            pi[s, 0, x] = lower
            pi[s, 1, x] = higher
        for c in corners:
            @pl.when(cthere[c])
            def _(c=c, s=s):
                first_d(s, c).start()
        for side in range(2):
            @pl.when(yside[side])
            def _(side=side, s=s):
                first_y(s, side).start()

    def mix(c, e, v):
        return c + 2.0 * c * e, c * jnp.sqrt(2.0 * v + 1.0), c

    for x in range(tx):
        parts = mix(raw[0, x], raw[1, x], raw[2, x])
        for n in range(3):
            cg[n, PAIR + x] = parts[n]

    for table in tables:
        table.wait()
    tile = 2 * ROWS
    wide = (width * ROWS + tile - 1) // tile
    count = lax.broadcasted_iota(jnp.int32, (tile, nrec), 0)
    level = lax.broadcasted_iota(jnp.int32, (nz, nrec), 0)
    for r in range(waves):
        px = positions[0, r:r + 1, :] - (a * tx - lead)
        qy = positions[1, r:r + 1, :] - (b * ty + hp * ROWS)
        pz = positions[2, r:r + 1, :]
        column = (px >= 0) & (px < width)
        within = (qy >= 0) & (qy < ROWS)
        cell = jnp.where(column & within, px * ROWS + qy, -1)
        brim = jnp.where(column & (qy == ROWS), px * ROWS, jnp.where(column & (qy == -1), px * ROWS + ROWS - 1, -1))
        core = jnp.where((px >= lead) & (px < lead + tx) & within, (px - lead) * ROWS + qy, -1)
        for ref, where, parts in ((pickg, cell, wide), (pickh, brim, wide), (pickb, core, tx * ROWS // tile)):
            for n in range(parts):
                ref[r, pl.ds(n * tile, tile), :] = jnp.where(count + n * tile == where, 1.0, 0.0).astype(bf16)
        where_z = jnp.where(level == pz, 1.0, 0.0).T.astype(bf16)
        spot[r, pl.ds(0, nrec), :] = where_z
        spot[r, pl.ds(nrec, nrec), :] = where_z

    def blank(j, carry):
        for r in range(waves):
            for x in range(HMAX):
                snaps[j, r, x] = zero
                snaps[j, r, HMAX + tx + x] = zero
        return carry

    lax.fori_loop(0, blocks, blank, 0)

    def inject(turn_index, r):
        def strength(moment):
            s = jnp.broadcast_to(amplitudes[r, pl.ds(moment, 1), :], (tile, nrec))
            high = s.astype(bf16)
            low = (s - high.astype(f32)).astype(bf16)
            return high, low

        def weigh(ref, n, parts):
            p = ref[r, pl.ds(n * tile, tile), :]
            return jnp.concatenate([p * parts[0], p * parts[1]], axis=1)

        one, two = strength(PAIR * turn_index), strength(PAIR * turn_index + 1)
        rows = [weigh(pickg, n, one) for n in range(wide)] + [weigh(pickh, n, one) for n in range(wide)]
        rows += [weigh(pickb, n, two) for n in range(tx * ROWS // tile)]
        found = jnp.dot(jnp.concatenate(rows, axis=0), spot[r], preferred_element_type=f32)
        injg[r] = found[:wide * tile]
        injh[r] = found[wide * tile:2 * wide * tile]
        injb[r] = found[2 * wide * tile:]

    def down(v):
        tiles = [v[:, n * LANES:(n + 1) * LANES] for n in range(nz // LANES)]
        fore = [turn(t, 1, 1) for t in tiles]
        back = [turn(t, -1, 1) for t in tiles]
        sums = []
        for n, t in enumerate(tiles):
            before = jnp.where(lane == 0, fore[n - 1] if n else 0.0, fore[n])
            after = jnp.where(lane == LANES - 1, back[n + 1] if n + 1 < len(tiles) else 0.0, back[n])
            sums.append(before + after - 2.0 * t)
        return jnp.concatenate(sums, axis=1)

    def advance(r, now, base, order, brim, gref, href):
        then = 1 - now

        def row_of(w, deep=True):
            slot = base + w
            return [sg[r, now, 0, slot]] + ([sh[r, now, 0, slot]] if deep else [])

        last = None
        for w in order:
            slot = base + w
            if last is not None and w == last + 1:
                behind, here = here, ahead
            else:
                behind, here = row_of(w - 1, brim), row_of(w)
            ahead = row_of(w + 1)
            last = w
            ups, downs = [turn(t, 1) for t in here], [turn(t, -1) for t in here]
            for n in range(2 if brim else 1):
                grid, coefs, source = (sh, ch, href) if n else (sg, cg, gref)
                north = jnp.where(top, ups[1 - n], ups[n])
                south = jnp.where(bottom, downs[1 - n], downs[n])
                m = here[n]
                across = (north + south) + (behind[n] + ahead[n]) - 4.0 * m
                aux = grid[r, now, 1, slot]
                vertical = down(aux)
                extra = source[r, pl.ds(w * ROWS, ROWS), :]
                hor, cpl, ver = (coefs[k, slot] for k in range(3))
                grid[r, then, 0, slot] = 2.0 * m - grid[r, then, 0, slot] + hor * across + cpl * vertical + extra
                grid[r, then, 1, slot] = 2.0 * aux - grid[r, then, 1, slot] + cpl * across + ver * vertical + extra

    def first_merge(s):
        for side in range(2):
            @pl.when(yside[side])
            def _(side=side):
                first_y(s, side, True).wait_recv()
                first_y(s, side).wait_send()
        for c in corners:
            @pl.when(cthere[c])
            def _(c=c):
                first_d(s, c, True).wait_recv()
                first_d(s, c).wait_send()

        for x in range(tx):
            below, above = iy[s, 0, x], iy[s, 1, x]

            def field(n, below=below, above=above):
                if n == 0:
                    return jnp.where(upper, above, below)
                return jnp.where(upper, turn(above, -n - 1), turn(below, n + 1))

            for n in range(4):
                sh[2 * s, n // 2, n % 2, PAIR + x] = field(n)
            if s == 0:
                parts = mix(*(jnp.where(top | bottom, field(4 + n), 0.0) for n in range(3)))
                for n in range(3):
                    ch[n, PAIR + x] = parts[n]
        for side in range(2):
            @pl.when(xside[side])
            def _(side=side):
                for group, n in firsts:
                    if group == s or (s == 0 and group == shots):
                        first_x(side, group, n, True).wait_recv()
                        first_x(side, group, n).wait_send()
                near, low = (right, right) if side else (1, 0)
                for n in range(PAIR):
                    sg[2 * s, 0, 0, low + n] = ix[side, s, n]
                for n in range(1, 4):
                    sg[2 * s, n // 2, n % 2, near] = ix[side, s, n + 1]
                sh[2 * s, 0, 0, near] = jnp.where(upper, idg[s, side, 1], idg[s, side, 0])
                if s == 0:
                    parts = mix(ixc[side, 0], ixc[side, 1], ixc[side, 2])
                    for n in range(3):
                        cg[n, near] = parts[n]

    def halo_x(slot, r, side, n, arrival=False):
        if n == 0:
            rows, target = pl.ds(right - PAIR if side else PAIR, PAIR), pl.ds(0, PAIR)
        else:
            rows, target = pl.ds(right - 1 if side else PAIR, 1), pl.ds(PAIR, 1)
        into = side if arrival else 1 - side
        target = rx.at[slot, r, into, target]
        return pltpu.make_async_remote_copy(
            src_ref=target if arrival else sg.at[r, 0, n, rows], dst_ref=target, send_sem=hsx.at[slot, r, side, n],
            recv_sem=hrx.at[slot, r, into, n], device_id=xdev[side], device_id_type=MESH,
        )

    def halo_y(slot, r, side, strip, arrival=False):
        into = side if arrival else 1 - side
        target = ry.at[slot, r, into, strip]
        return pltpu.make_async_remote_copy(
            src_ref=target if arrival else py.at[r, side, strip], dst_ref=target, send_sem=hsy.at[slot, r, side, strip],
            recv_sem=hry.at[slot, r, into, strip], device_id=ydev[side], device_id_type=MESH,
        )

    def halo_d(slot, r, corner, arrival=False):
        i, j = corner
        u, v = corner if arrival else (1 - i, 1 - j)
        target = rd.at[slot, r, u, v]
        return pltpu.make_async_remote_copy(
            src_ref=target if arrival else pc.at[r, i, j], dst_ref=target,
            send_sem=hsd.at[slot, r, i, j], recv_sem=hrd.at[slot, r, u, v], device_id=cdev[corner],
            device_id_type=MESH,
        )

    def corner(slot, r, side):
        above, below = (jnp.broadcast_to(rd[slot, r, side, n], (ROWS, nz)) for n in (1, 0))
        return jnp.where(upper, above, below)

    def merge(slot, r):
        for side in range(2):
            @pl.when(yside[side])
            def _(side=side):
                for strip in range(strips):
                    halo_y(slot, r, side, strip, True).wait_recv()
                    halo_y(slot, r, side, strip).wait_send()
        for x in range(tx):
            strip, w = x // ROWS, x % ROWS
            n, k = w // quad, w % quad
            below, above = ry[slot, r, 0, strip, n], ry[slot, r, 1, strip, n]
            sh[r, 0, 0, PAIR + x] = jnp.where(upper, turn(above, -PAIR * k), turn(below, -PAIR * (k + 1)))
            below, above = ry[slot, r, 0, strip, PAIR], ry[slot, r, 1, strip, PAIR]
            sh[r, 0, 1, PAIR + x] = jnp.where(upper, turn(above, -w), turn(below, -w - 1))
        for c in corners:
            @pl.when(cthere[c])
            def _(c=c):
                halo_d(slot, r, c, True).wait_recv()
                halo_d(slot, r, c).wait_send()
        for side in range(2):
            @pl.when(xside[side])
            def _(side=side):
                for n in range(2):
                    halo_x(slot, r, side, n, True).wait_recv()
                    halo_x(slot, r, side, n).wait_send()
                near, low = (right, right) if side else (1, 0)
                for n in range(PAIR):
                    sg[r, 0, 0, low + n] = rx[slot, r, side, n]
                sg[r, 0, 1, near] = rx[slot, r, side, PAIR]
                sh[r, 0, 0, near] = corner(slot, r, side)

    def send_x(slot, r):
        for i, j in corners:
            v = sg[r, 0, 0, right - 1 if i else PAIR]
            pc[r, i, j] = v[ROWS - 1:] if j else v[:1]
        for c in corners:
            @pl.when(cthere[c])
            def _(c=c):
                halo_d(slot, r, c).start()
        for side in range(2):
            @pl.when(xside[side])
            def _(side=side):
                for n in range(2):
                    halo_x(slot, r, side, n).start()

    def send_y(slot, r, strip):
        for n in range(packs):
            field, size, first = (0, PAIR, n * quad) if n < PAIR else (1, 1, 0)
            lower = higher = None
            for k in range(ROWS // size):
                v = sg[r, 0, field, PAIR + strip * ROWS + first + k]
                one, two = turn(v, size * k), turn(v, size * (k + 1))
                lower = one if k == 0 else jnp.where(row < size * k, lower, one)
                higher = two if k == 0 else jnp.where(row < size * k, higher, two)
            py[r, 0, strip, n] = lower
            py[r, 1, strip, n] = higher
        for side in range(2):
            @pl.when(yside[side])
            def _(side=side):
                halo_y(slot, r, side, strip).start()

    def fringe_copy(j, s, side, skip, arrival=False):
        into = side if arrival else 1 - side
        both = pl.ds(2 * s, 2)
        target = fringe.at[j, into, both, pl.ds(0, HMAX - skip)]
        source = pl.ds(tx if side else HMAX + skip, HMAX - skip)
        return pltpu.make_async_remote_copy(
            src_ref=target if arrival else snaps.at[j, both, source], dst_ref=target, send_sem=xs.at[j, s, side],
            recv_sem=xr.at[j, s, into], device_id=xdev[side], device_id_type=MESH,
        )

    def send_fringe(j, s, skip):
        for side in range(2):
            @pl.when(xside[side])
            def _(side=side):
                fringe_copy(j, s, side, skip).start()

    def merge_fringe(j, skip):
        for s in range(shots):
            for side in range(2):
                @pl.when(xside[side])
                def _(side=side, s=s):
                    fringe_copy(j, s, side, skip, True).wait_recv()
                    fringe_copy(j, s, side, skip).wait_send()
                    for r in range(2 * s, 2 * s + 2):
                        for x in range(HMAX - skip):
                            snaps[j, r, side * (HMAX + tx + skip) + x] = fringe[j, side, r, x]

    def keep_halo(e, r):
        for side in range(2):
            @pl.when(xside[side])
            def _(side=side):
                for n in range(PAIR):
                    snaps[e // per - 1, r, (HMAX + tx if side else HMAX - PAIR) + n] = rx[e % 2, r, side, n]

    brink = list(range(PAIR)) + list(range(tx - PAIR, tx))
    rest = [[x for x in range(n * ROWS, (n + 1) * ROWS) if x not in brink] for n in range(strips)]

    def cycle(e, carry):
        for r in range(waves):
            inject(e, r)

        for r in range(waves):
            if r % 2 == 0:
                @pl.when(e == 0)
                def _(r=r):
                    first_merge(r // 2)

            @pl.when(e > 0)
            def _(r=r):
                merge(e % 2, r)

            @pl.when((e % per == 0) & (e > 0))
            def _(r=r):
                keep_halo(e, r)

            advance(r, 0, start, range(width), True, injg, injh)
            advance(r, 1, PAIR, brink, False, injb, None)

            @pl.when(e < turns - 1)
            def _(r=r):
                send_x((e + 1) % 2, r)

            for strip in range(strips):
                advance(r, 1, PAIR, rest[strip], False, injb, None)

                @pl.when(e < turns - 1)
                def _(r=r, strip=strip):
                    send_y((e + 1) % 2, r, strip)

            if r % 2 == 1:
                @pl.when(e % per == per - 1)
                def _(r=r):
                    for n in (r - 1, r):
                        for x in range(tx):
                            snaps[e // per, n, HMAX + x] = sg[n, 0, 0, PAIR + x]

                @pl.when(e == turns - 1)
                def _(r=r):
                    send_fringe(blocks - 1, r // 2, 0)

        @pl.when((e % per == per - 1) & (e < turns - 1))
        def _():
            send_fringe(e // per, 0, PAIR)

        @pl.when((e % per == 0) & (e > 0))
        def _():
            for s in range(1, shots):
                send_fringe(e // per - 1, s, PAIR)

        return carry

    lax.fori_loop(0, turns, cycle, 0)

    def swap_copy(n, rows, part):
        return pltpu.make_async_remote_copy(
            src_ref=outgoing.at[n, rows], dst_ref=out.at[n, rows, mine, :], send_sem=gs.at[part, n],
            recv_sem=gr.at[part, n], device_id=partner, device_id_type=MESH,
        )

    def product(shift, x):
        sums = None
        for j in range(blocks):
            for s in range(shots):
                term = snaps[j, 2 * s, HMAX - shift + x] * snaps[j, 2 * s + 1, HMAX + shift + x]
                sums = term if sums is None else sums + term
        return sums

    mid = tx // 2
    spans = [pl.ds(a * mid, mid), pl.ds((1 - a) * mid, mid)] if nx == 2 else [pl.ds(0, mid), pl.ds(mid, mid)]
    for part, rows in enumerate(spans):
        if part == (1 if nx == 2 else 0):
            def earlier(j, carry):
                merge_fringe(j, PAIR)
                return carry

            lax.fori_loop(0, blocks - 1, earlier, 0)
            merge_fringe(blocks - 1, 0)

        def theirs(n, carry, part=part, rows=rows):
            shift = offsets[pair * own + (1 - half) * own + n]
            for x in range(mid):
                outgoing[n, rows.start + x] = product(shift, rows.start + x)
            swap_copy(n, rows, part).start()
            return carry

        lax.fori_loop(0, own, theirs, 0)

    def ours(n, carry):
        shift = offsets[pair * own + half * own + n]
        for x in range(tx):
            out[n, x, mine, :] = product(shift, x)
        return carry

    lax.fori_loop(0, own, ours, 0)
    for part, rows in enumerate(spans):
        def done(n, carry, part=part, rows=rows):
            swap_copy(n, rows, part).wait_recv()
            swap_copy(n, rows, part).wait_send()
            return carry

        lax.fori_loop(0, own, done, 0)


def shards(sizes, checkpoint, courant, epsilon, delta, positions, amplitudes, offsets):
    ng, nx, ny = sizes
    shots = checkpoint.shape[0]
    waves = 2 * shots
    tx, ty, nz = courant.shape
    nrec = positions.shape[2]
    steps = amplitudes.shape[1]
    blocks = steps // SNAP
    nh = offsets.shape[0]
    own = nh // ng
    assert ng % 2 == 0 and ty == 2 * ROWS and tx == 2 * HMAX and nz % LANES == 0 and nh % ng == 0 and nx > 1
    assert shots <= 2 and steps % SNAP == 0
    width = tx + (1 if nx == 2 else 2)
    wide = (width + 1) // 2 * 2 * ROWS
    slots = tx + 2 * PAIR
    packs, strips = PAIR + 1, tx // ROWS
    f32, bf16 = jnp.float32, jnp.bfloat16
    dma = pltpu.SemaphoreType.DMA
    vmem = pl.BlockSpec(memory_space=pltpu.VMEM)

    places = positions.transpose(1, 0, 2)
    arguments = (courant, epsilon, delta, checkpoint, places, amplitudes, offsets)

    def held(*shape, dtype=f32):
        return pltpu.VMEM(shape, dtype)

    return pl.pallas_call(
        functools.partial(kernel, sizes),
        out_shape=jax.ShapeDtypeStruct((own, tx, ty, nz), f32),
        in_specs=[pl.BlockSpec(memory_space=pltpu.HBM)] * 7,
        out_specs=vmem,
        scratch_shapes=[
            held(*places.shape, dtype=places.dtype),
            held(*amplitudes.shape),
            pltpu.SMEM(offsets.shape, offsets.dtype),
            held(waves, 2, 2, slots, ROWS, nz),
            held(waves, 2, 2, slots, ROWS, nz),
            held(3, tx, ROWS, nz),
            held(3, slots, ROWS, nz),
            held(3, slots, ROWS, nz),
            held(waves, wide, nrec, dtype=bf16),
            held(waves, wide, nrec, dtype=bf16),
            held(waves, tx * ROWS, nrec, dtype=bf16),
            held(waves, 2 * nrec, nz, dtype=bf16),
            held(waves, wide, nz),
            held(waves, wide, nz),
            held(waves, tx * ROWS, nz),
            held(2, shots, PAIR + 3, ROWS, nz),
            held(2, 3, ROWS, nz),
            held(shots, 2, tx, ROWS, nz),
            held(shots, 2, 2, ROWS, nz),
            held(shots, 2, tx, ROWS, nz),
            held(waves, 2, strips, packs, ROWS, nz),
            held(waves, 2, 2, 1, nz),
            held(2, waves, 2, PAIR + 1, ROWS, nz),
            held(2, waves, 2, strips, packs, ROWS, nz),
            held(2, waves, 2, 2, 1, nz),
            held(blocks, waves, tx + 2 * HMAX, ROWS, nz),
            held(blocks, 2, waves, HMAX, ROWS, nz),
            held(own, tx, ROWS, nz),
            dma((6 + 4 * shots,)),
            dma((2, shots + 1, 4)),
            dma((2, shots + 1, 4)),
            dma((shots, 2)),
            dma((shots, 2)),
            dma((shots, 2, 2)),
            dma((shots, 2, 2)),
            dma((2, waves, 2, 2)),
            dma((2, waves, 2, 2)),
            dma((2, waves, 2, strips)),
            dma((2, waves, 2, strips)),
            dma((2, waves, 2, 2)),
            dma((2, waves, 2, 2)),
            dma((blocks, shots, 2)),
            dma((blocks, shots, 2)),
            dma((2, own)),
            dma((2, own)),
        ],
        compiler_params=pltpu.CompilerParams(
            collective_id=0, has_side_effects=True, vmem_limit_bytes=44 * 1024 * 1024
        ),
    )(*(pltpu.with_memory_space_constraint(v, pltpu.HBM) for v in arguments))


def solution(mesh):
    sizes = tuple(mesh.shape[axis] for axis in ("grp", "gx", "gy"))
    return jax.shard_map(
        functools.partial(shards, sizes),
        mesh=mesh,
        in_specs=(
            P(None, None, None, "gx", "gy", None),
            P("gx", "gy", None),
            P("gx", "gy", None),
            P("gx", "gy", None),
            P(),
            P(),
            P(),
        ),
        out_specs=P("grp", "gx", "gy", None),
        check_vma=False,
    )
```

```python
import functools
import jax
import jax.numpy as jnp
from jax import lax
from jax.experimental import pallas as pl
from jax.experimental.pallas import tpu as pltpu
from jax.sharding import PartitionSpec as P

SNAP = 4
HMAX = 8
PAIR = 2
ROWS = 8
LANES = 128
MESH = pl.DeviceIdType.MESH


def kernel(sizes, courant, epsilon, delta, checkpoint, places, weights, shifts, out,
           positions, amplitudes, offsets, sg, sh, raw, cg, ch, pickg, pickh, pickb, spot, injg, injh, injb, ix, ixc, iy, idg, pi, py, pc, rx, ry, rd,
           snaps, fringe, outgoing,
           ls, isx, irx, isy, iry, isd, ird, hsx, hrx, hsy, hry, hsd, hrd, xs, xr, gs, gr):
    ng, nx, ny = sizes
    shots = checkpoint.shape[0]
    waves = 2 * shots
    tx, ty, nz = courant.shape
    nrec = positions.shape[2]
    steps = amplitudes.shape[1]
    own = offsets.shape[0] // ng
    turns = steps // PAIR
    blocks = steps // SNAP
    per = SNAP // PAIR
    d, a, b = lax.axis_index("grp"), lax.axis_index("gx"), lax.axis_index("gy")
    half = d % 2
    pair = d - half
    other = pair + 1 - half
    flip = b % 2
    hp = half + flip - 2 * half * flip
    partner = {"grp": other, "gx": a, "gy": b}
    width = tx + (1 if nx == 2 else 2)
    lead = a if nx == 2 else 1
    start = PAIR - lead
    right = PAIR + tx
    f32, bf16 = jnp.float32, jnp.bfloat16
    mine = pl.ds(pl.multiple_of(hp * ROWS, ROWS), ROWS)

    inner = (hp, 1 - hp)
    xside = (a > 0, a < nx - 1)
    yside = ((hp == 1) | (b > 0), (hp == 0) | (b < ny - 1))
    near_y = tuple((d + inner[i] * (other - d), b + (2 * i - 1) * (1 - inner[i])) for i in range(2))
    xdev = tuple({"grp": d, "gx": a + 2 * i - 1, "gy": b} for i in range(2))
    ydev = tuple({"grp": near_y[i][0], "gx": a, "gy": near_y[i][1]} for i in range(2))
    corners = [(i, j) for i in range(2) for j in range(2)]
    cthere = {(i, j): xside[i] & yside[j] for i, j in corners}
    cdev = {(i, j): {"grp": near_y[j][0], "gx": a + 2 * i - 1, "gy": near_y[j][1]} for i, j in corners}

    barrier = pltpu.get_barrier_semaphore()
    met = [(xside[i], xdev[i]) for i in range(2)] + [(yside[i], ydev[i]) for i in range(2)]
    met += [(cthere[c], cdev[c]) for c in corners]
    pl.semaphore_signal(barrier, inc=1, device_id=partner, device_id_type=MESH)
    for there, device in met:
        @pl.when(there)
        def _(device=device):
            pl.semaphore_signal(barrier, inc=1, device_id=device, device_id_type=MESH)

    models = (courant, epsilon, delta)

    def model_load(n):
        return pltpu.make_async_copy(models[n].at[:, mine, :], raw.at[n], ls.at[n])

    def state_load(s, moment, field):
        return pltpu.make_async_copy(
            checkpoint.at[s, moment, field, :, mine, :], sg.at[2 * s, moment, field, pl.ds(PAIR, tx)],
            ls.at[3 + 4 * s + 2 * moment + field],
        )

    loads = [(s, moment, field) for s in range(shots) for moment in range(2) for field in range(2)]
    tables = [
        pltpu.make_async_copy(source, target, ls.at[3 + 4 * shots + n])
        for n, (source, target) in enumerate(((places, positions), (weights, amplitudes), (shifts, offsets)))
    ]
    for n in range(3):
        model_load(n).start()
    for load in loads:
        state_load(*load).start()
    for table in tables:
        table.start()

    zero = jnp.zeros((ROWS, nz), f32)
    row = lax.broadcasted_iota(jnp.int32, (ROWS, nz), 0)
    lane = lax.broadcasted_iota(jnp.int32, (ROWS, LANES), 1)
    top, bottom, upper = row == 0, row == ROWS - 1, row < ROWS // 2

    def turn(v, shift, axis=0):
        shift = shift % v.shape[axis]
        return v if shift == 0 else pltpu.roll(v, shift, axis)

    outer = (0, 1, right, right + 1)
    quad, packs, strips = ROWS // PAIR, PAIR + 1, tx // ROWS

    def wipe(x, carry):
        for r in range(waves):
            for moment in range(2):
                for field in range(2):
                    if r % 2:
                        sg[r, moment, field, x] = zero
                    sh[r, moment, field, x] = zero
        return carry

    lax.fori_loop(0, tx + 2 * PAIR, wipe, 0)
    for x in outer:
        for s in range(shots):
            for moment in range(2):
                for field in range(2):
                    sg[2 * s, moment, field, x] = zero
        for n in range(3):
            cg[n, x] = zero
            ch[n, x] = zero
    for side in range(2):
        @pl.when(jnp.logical_not(yside[side]))
        def _(side=side):
            for x in range(tx):
                for s in range(shots):
                    iy[s, side, x] = zero
            for slot in range(2):
                for r in range(waves):
                    for strip in range(strips):
                        for n in range(packs):
                            ry[slot, r, side, strip, n] = zero
    for i, j in corners:
        @pl.when(jnp.logical_not(cthere[i, j]))
        def _(i=i, j=j):
            for s in range(shots):
                idg[s, i, j] = zero
            for slot in range(2):
                for r in range(waves):
                    rd[slot, r, i, j] = zero[:1]

    total = 1
    for there, _ in met:
        total = total + there.astype(jnp.int32)
    pl.semaphore_wait(barrier, total)

    def first_x(side, s, n, arrival=False):
        last = pl.ds(tx - 1 if side else 0, 1)
        into = side if arrival else 1 - side
        if s < shots:
            rows = pl.ds(tx - PAIR if side else 0, PAIR) if n == 0 else last
            source = checkpoint.at[s, n // 2, n % 2, rows, mine, :]
            target = ix.at[into, s, pl.ds(0, PAIR) if n == 0 else pl.ds(n + 1, 1)]
        else:
            source, target = models[n].at[last, mine, :], ixc.at[into, pl.ds(n, 1)]
        return pltpu.make_async_remote_copy(
            src_ref=target if arrival else source, dst_ref=target, send_sem=isx.at[side, s, n],
            recv_sem=irx.at[into, s, n], device_id=xdev[side], device_id_type=MESH,
        )

    firsts = [(shots, n) for n in range(3)] + [(s, n) for s in range(shots) for n in range(4)]
    for side in range(2):
        @pl.when(xside[side])
        def _(side=side):
            for s, n in firsts:
                first_x(side, s, n).start()

    for n in range(3):
        model_load(n).wait()
    for load in loads:
        state_load(*load).wait()

    def first_y(s, side, arrival=False):
        into = side if arrival else 1 - side
        return pltpu.make_async_remote_copy(
            src_ref=iy.at[s, into] if arrival else pi.at[s, side], dst_ref=iy.at[s, into], send_sem=isy.at[s, side],
            recv_sem=iry.at[s, into], device_id=ydev[side], device_id_type=MESH,
        )

    def first_d(s, corner, arrival=False):
        i, j = corner
        u, v = corner if arrival else (1 - i, 1 - j)
        return pltpu.make_async_remote_copy(
            src_ref=idg.at[s, u, v] if arrival else pi.at[s, j, tx - 1 if i else 0], dst_ref=idg.at[s, u, v],
            send_sem=isd.at[s, i, j], recv_sem=ird.at[s, u, v], device_id=cdev[corner], device_id_type=MESH,
        )

    for s in range(shots):
        for x in range(tx):
            tiles = [sg[2 * s, n // 2, n % 2, PAIR + x] for n in range(4)]
            tiles += [raw[n, x] for n in range(3)] if s == 0 else []
            lower = higher = tiles[0]
            for n in range(1, len(tiles)):
                lower = jnp.where(row == n + 1, turn(tiles[n], n + 1), lower)
                higher = jnp.where(row == ROWS - 2 - n, turn(tiles[n], -n - 1), higher)
            pi[s, 0, x] = lower
            pi[s, 1, x] = higher
        for c in corners:
            @pl.when(cthere[c])
            def _(c=c, s=s):
                first_d(s, c).start()
        for side in range(2):
            @pl.when(yside[side])
            def _(side=side, s=s):
                first_y(s, side).start()

    def mix(c, e, v):
        return c + 2.0 * c * e, c * jnp.sqrt(2.0 * v + 1.0), c

    for x in range(tx):
        parts = mix(raw[0, x], raw[1, x], raw[2, x])
        for n in range(3):
            cg[n, PAIR + x] = parts[n]

    for table in tables:
        table.wait()
    tile = 2 * ROWS
    wide = (width * ROWS + tile - 1) // tile
    count = lax.broadcasted_iota(jnp.int32, (tile, nrec), 0)
    level = lax.broadcasted_iota(jnp.int32, (nz, nrec), 0)
    for r in range(waves):
        px = positions[0, r:r + 1, :] - (a * tx - lead)
        qy = positions[1, r:r + 1, :] - (b * ty + hp * ROWS)
        pz = positions[2, r:r + 1, :]
        column = (px >= 0) & (px < width)
        within = (qy >= 0) & (qy < ROWS)
        cell = jnp.where(column & within, px * ROWS + qy, -1)
        brim = jnp.where(column & (qy == ROWS), px * ROWS, jnp.where(column & (qy == -1), px * ROWS + ROWS - 1, -1))
        core = jnp.where((px >= lead) & (px < lead + tx) & within, (px - lead) * ROWS + qy, -1)
        for ref, where, parts in ((pickg, cell, wide), (pickh, brim, wide), (pickb, core, tx * ROWS // tile)):
            for n in range(parts):
                ref[r, pl.ds(n * tile, tile), :] = jnp.where(count + n * tile == where, 1.0, 0.0).astype(bf16)
        where_z = jnp.where(level == pz, 1.0, 0.0).T.astype(bf16)
        spot[r, pl.ds(0, nrec), :] = where_z
        spot[r, pl.ds(nrec, nrec), :] = where_z

    def blank(j, carry):
        for r in range(waves):
            for x in range(HMAX):
                snaps[j, r, x] = zero
                snaps[j, r, HMAX + tx + x] = zero
        return carry

    lax.fori_loop(0, blocks, blank, 0)

    def inject(turn_index, r):
        def strength(moment):
            s = jnp.broadcast_to(amplitudes[r, pl.ds(moment, 1), :], (tile, nrec))
            high = s.astype(bf16)
            low = (s - high.astype(f32)).astype(bf16)
            return high, low

        def weigh(ref, n, parts):
            p = ref[r, pl.ds(n * tile, tile), :]
            return jnp.concatenate([p * parts[0], p * parts[1]], axis=1)

        one, two = strength(PAIR * turn_index), strength(PAIR * turn_index + 1)
        rows = [weigh(pickg, n, one) for n in range(wide)] + [weigh(pickh, n, one) for n in range(wide)]
        rows += [weigh(pickb, n, two) for n in range(tx * ROWS // tile)]
        found = jnp.dot(jnp.concatenate(rows, axis=0), spot[r], preferred_element_type=f32)
        injg[r] = found[:wide * tile]
        injh[r] = found[wide * tile:2 * wide * tile]
        injb[r] = found[2 * wide * tile:]

    def down(v):
        tiles = [v[:, n * LANES:(n + 1) * LANES] for n in range(nz // LANES)]
        fore = [turn(t, 1, 1) for t in tiles]
        back = [turn(t, -1, 1) for t in tiles]
        sums = []
        for n, t in enumerate(tiles):
            before = jnp.where(lane == 0, fore[n - 1] if n else 0.0, fore[n])
            after = jnp.where(lane == LANES - 1, back[n + 1] if n + 1 < len(tiles) else 0.0, back[n])
            sums.append(before + after - 2.0 * t)
        return jnp.concatenate(sums, axis=1)

    def advance(r, now, base, order, brim, gref, href):
        then = 1 - now

        def row_of(w, deep=True):
            slot = base + w
            return [sg[r, now, 0, slot]] + ([sh[r, now, 0, slot]] if deep else [])

        last = None
        for w in order:
            slot = base + w
            if last is not None and w == last + 1:
                behind, here = here, ahead
            else:
                behind, here = row_of(w - 1, brim), row_of(w)
            ahead = row_of(w + 1)
            last = w
            ups, downs = [turn(t, 1) for t in here], [turn(t, -1) for t in here]
            for n in range(2 if brim else 1):
                grid, coefs, source = (sh, ch, href) if n else (sg, cg, gref)
                north = jnp.where(top, ups[1 - n], ups[n])
                south = jnp.where(bottom, downs[1 - n], downs[n])
                m = here[n]
                across = (north + south) + (behind[n] + ahead[n]) - 4.0 * m
                aux = grid[r, now, 1, slot]
                vertical = down(aux)
                extra = source[r, pl.ds(w * ROWS, ROWS), :]
                hor, cpl, ver = (coefs[k, slot] for k in range(3))
                grid[r, then, 0, slot] = 2.0 * m - grid[r, then, 0, slot] + hor * across + cpl * vertical + extra
                grid[r, then, 1, slot] = 2.0 * aux - grid[r, then, 1, slot] + cpl * across + ver * vertical + extra

    def first_merge(s):
        for side in range(2):
            @pl.when(yside[side])
            def _(side=side):
                first_y(s, side, True).wait_recv()
                first_y(s, side).wait_send()
        for c in corners:
            @pl.when(cthere[c])
            def _(c=c):
                first_d(s, c, True).wait_recv()
                first_d(s, c).wait_send()

        for x in range(tx):
            below, above = iy[s, 0, x], iy[s, 1, x]

            def field(n, below=below, above=above):
                if n == 0:
                    return jnp.where(upper, above, below)
                return jnp.where(upper, turn(above, -n - 1), turn(below, n + 1))

            for n in range(4):
                sh[2 * s, n // 2, n % 2, PAIR + x] = field(n)
            if s == 0:
                parts = mix(*(jnp.where(top | bottom, field(4 + n), 0.0) for n in range(3)))
                for n in range(3):
                    ch[n, PAIR + x] = parts[n]
        for side in range(2):
            @pl.when(xside[side])
            def _(side=side):
                for group, n in firsts:
                    if group == s or (s == 0 and group == shots):
                        first_x(side, group, n, True).wait_recv()
                        first_x(side, group, n).wait_send()
                near, low = (right, right) if side else (1, 0)
                for n in range(PAIR):
                    sg[2 * s, 0, 0, low + n] = ix[side, s, n]
                for n in range(1, 4):
                    sg[2 * s, n // 2, n % 2, near] = ix[side, s, n + 1]
                sh[2 * s, 0, 0, near] = jnp.where(upper, idg[s, side, 1], idg[s, side, 0])
                if s == 0:
                    parts = mix(ixc[side, 0], ixc[side, 1], ixc[side, 2])
                    for n in range(3):
                        cg[n, near] = parts[n]

    def halo_x(slot, r, side, n, arrival=False):
        if n == 0:
            rows, target = pl.ds(right - PAIR if side else PAIR, PAIR), pl.ds(0, PAIR)
        else:
            rows, target = pl.ds(right - 1 if side else PAIR, 1), pl.ds(PAIR, 1)
        into = side if arrival else 1 - side
        target = rx.at[slot, r, into, target]
        return pltpu.make_async_remote_copy(
            src_ref=target if arrival else sg.at[r, 0, n, rows], dst_ref=target, send_sem=hsx.at[slot, r, side, n],
            recv_sem=hrx.at[slot, r, into, n], device_id=xdev[side], device_id_type=MESH,
        )

    def halo_y(slot, r, side, strip, arrival=False):
        into = side if arrival else 1 - side
        target = ry.at[slot, r, into, strip]
        return pltpu.make_async_remote_copy(
            src_ref=target if arrival else py.at[r, side, strip], dst_ref=target, send_sem=hsy.at[slot, r, side, strip],
            recv_sem=hry.at[slot, r, into, strip], device_id=ydev[side], device_id_type=MESH,
        )

    def halo_d(slot, r, corner, arrival=False):
        i, j = corner
        u, v = corner if arrival else (1 - i, 1 - j)
        target = rd.at[slot, r, u, v]
        return pltpu.make_async_remote_copy(
            src_ref=target if arrival else pc.at[r, i, j], dst_ref=target,
            send_sem=hsd.at[slot, r, i, j], recv_sem=hrd.at[slot, r, u, v], device_id=cdev[corner],
            device_id_type=MESH,
        )

    def corner(slot, r, side):
        above, below = (jnp.broadcast_to(rd[slot, r, side, n], (ROWS, nz)) for n in (1, 0))
        return jnp.where(upper, above, below)

    def merge(slot, r):
        for side in range(2):
            @pl.when(yside[side])
            def _(side=side):
                for strip in range(strips):
                    halo_y(slot, r, side, strip, True).wait_recv()
                    halo_y(slot, r, side, strip).wait_send()
        for x in range(tx):
            strip, w = x // ROWS, x % ROWS
            n, k = w // quad, w % quad
            below, above = ry[slot, r, 0, strip, n], ry[slot, r, 1, strip, n]
            sh[r, 0, 0, PAIR + x] = jnp.where(upper, turn(above, -PAIR * k), turn(below, -PAIR * (k + 1)))
            below, above = ry[slot, r, 0, strip, PAIR], ry[slot, r, 1, strip, PAIR]
            sh[r, 0, 1, PAIR + x] = jnp.where(upper, turn(above, -w), turn(below, -w - 1))
        for c in corners:
            @pl.when(cthere[c])
            def _(c=c):
                halo_d(slot, r, c, True).wait_recv()
                halo_d(slot, r, c).wait_send()
        for side in range(2):
            @pl.when(xside[side])
            def _(side=side):
                for n in range(2):
                    halo_x(slot, r, side, n, True).wait_recv()
                    halo_x(slot, r, side, n).wait_send()
                near, low = (right, right) if side else (1, 0)
                for n in range(PAIR):
                    sg[r, 0, 0, low + n] = rx[slot, r, side, n]
                sg[r, 0, 1, near] = rx[slot, r, side, PAIR]
                sh[r, 0, 0, near] = corner(slot, r, side)

    def send_x(slot, r):
        for i, j in corners:
            v = sg[r, 0, 0, right - 1 if i else PAIR]
            pc[r, i, j] = v[ROWS - 1:] if j else v[:1]
        for c in corners:
            @pl.when(cthere[c])
            def _(c=c):
                halo_d(slot, r, c).start()
        for side in range(2):
            @pl.when(xside[side])
            def _(side=side):
                for n in range(2):
                    halo_x(slot, r, side, n).start()

    def send_y(slot, r, strip):
        for n in range(packs):
            field, size, first = (0, PAIR, n * quad) if n < PAIR else (1, 1, 0)
            lower = higher = None
            for k in range(ROWS // size):
                v = sg[r, 0, field, PAIR + strip * ROWS + first + k]
                one, two = turn(v, size * k), turn(v, size * (k + 1))
                lower = one if k == 0 else jnp.where(row < size * k, lower, one)
                higher = two if k == 0 else jnp.where(row < size * k, higher, two)
            py[r, 0, strip, n] = lower
            py[r, 1, strip, n] = higher
        for side in range(2):
            @pl.when(yside[side])
            def _(side=side):
                halo_y(slot, r, side, strip).start()

    def fringe_copy(j, s, side, skip, arrival=False):
        into = side if arrival else 1 - side
        both = pl.ds(2 * s, 2)
        target = fringe.at[j, into, both, pl.ds(0, HMAX - skip)]
        source = pl.ds(tx if side else HMAX + skip, HMAX - skip)
        return pltpu.make_async_remote_copy(
            src_ref=target if arrival else snaps.at[j, both, source], dst_ref=target, send_sem=xs.at[j, s, side],
            recv_sem=xr.at[j, s, into], device_id=xdev[side], device_id_type=MESH,
        )

    def send_fringe(j, s, skip):
        for side in range(2):
            @pl.when(xside[side])
            def _(side=side):
                fringe_copy(j, s, side, skip).start()

    def merge_fringe(j, skip):
        for s in range(shots):
            for side in range(2):
                @pl.when(xside[side])
                def _(side=side, s=s):
                    fringe_copy(j, s, side, skip, True).wait_recv()
                    fringe_copy(j, s, side, skip).wait_send()
                    for r in range(2 * s, 2 * s + 2):
                        for x in range(HMAX - skip):
                            snaps[j, r, side * (HMAX + tx + skip) + x] = fringe[j, side, r, x]

    def keep_halo(e, r):
        for side in range(2):
            @pl.when(xside[side])
            def _(side=side):
                for n in range(PAIR):
                    snaps[e // per - 1, r, (HMAX + tx if side else HMAX - PAIR) + n] = rx[e % 2, r, side, n]

    queue = [0, 1] + [r for s in range(1, shots) for r in (2 * s + 1, 2 * s)]
    brink = list(range(PAIR)) + list(range(tx - PAIR, tx))
    rest = [[x for x in range(n * ROWS, (n + 1) * ROWS) if x not in brink] for n in range(strips)]

    def cycle(e, carry):
        for r in range(waves):
            inject(e, r)

        for place, r in enumerate(queue):
            if r % 2 == 0:
                @pl.when(e == 0)
                def _(r=r):
                    first_merge(r // 2)

            @pl.when(e > 0)
            def _(r=r):
                merge(e % 2, r)

            @pl.when((e % per == 0) & (e > 0))
            def _(r=r):
                keep_halo(e, r)

            advance(r, 0, start, range(width), True, injg, injh)
            advance(r, 1, PAIR, brink, False, injb, None)

            @pl.when(e < turns - 1)
            def _(r=r):
                send_x((e + 1) % 2, r)

            for strip in range(strips):
                advance(r, 1, PAIR, rest[strip], False, injb, None)

                @pl.when(e < turns - 1)
                def _(r=r, strip=strip):
                    send_y((e + 1) % 2, r, strip)

            if place % 2 == 1:
                @pl.when(e % per == per - 1)
                def _(r=r):
                    for n in (r - r % 2, r - r % 2 + 1):
                        for x in range(tx):
                            snaps[e // per, n, HMAX + x] = sg[n, 0, 0, PAIR + x]

                @pl.when(e == turns - 1)
                def _(r=r):
                    send_fringe(blocks - 1, r // 2, 0)

        @pl.when((e % per == per - 1) & (e < turns - 1))
        def _():
            send_fringe(e // per, 0, PAIR)

        @pl.when((e % per == 0) & (e > 0))
        def _():
            for s in range(1, shots):
                send_fringe(e // per - 1, s, PAIR)

        return carry

    lax.fori_loop(0, turns, cycle, 0)

    def swap_copy(n, rows, part):
        return pltpu.make_async_remote_copy(
            src_ref=outgoing.at[n, rows], dst_ref=out.at[n, rows, mine, :], send_sem=gs.at[part, n],
            recv_sem=gr.at[part, n], device_id=partner, device_id_type=MESH,
        )

    def product(shift, x):
        sums = None
        for j in range(blocks):
            for s in range(shots):
                term = snaps[j, 2 * s, HMAX - shift + x] * snaps[j, 2 * s + 1, HMAX + shift + x]
                sums = term if sums is None else sums + term
        return sums

    mid = tx // 2
    spans = [pl.ds(a * mid, mid), pl.ds((1 - a) * mid, mid)] if nx == 2 else [pl.ds(0, mid), pl.ds(mid, mid)]
    for part, rows in enumerate(spans):
        if part == (1 if nx == 2 else 0):
            def earlier(j, carry):
                merge_fringe(j, PAIR)
                return carry

            lax.fori_loop(0, blocks - 1, earlier, 0)
            merge_fringe(blocks - 1, 0)

        def theirs(n, carry, part=part, rows=rows):
            shift = offsets[pair * own + (1 - half) * own + n]
            for x in range(mid):
                outgoing[n, rows.start + x] = product(shift, rows.start + x)
            swap_copy(n, rows, part).start()
            return carry

        lax.fori_loop(0, own, theirs, 0)

    def ours(n, carry):
        shift = offsets[pair * own + half * own + n]
        for x in range(tx):
            out[n, x, mine, :] = product(shift, x)
        return carry

    lax.fori_loop(0, own, ours, 0)
    for part, rows in enumerate(spans):
        def done(n, carry, part=part, rows=rows):
            swap_copy(n, rows, part).wait_recv()
            swap_copy(n, rows, part).wait_send()
            return carry

        lax.fori_loop(0, own, done, 0)


def shards(sizes, checkpoint, courant, epsilon, delta, positions, amplitudes, offsets):
    ng, nx, ny = sizes
    shots = checkpoint.shape[0]
    waves = 2 * shots
    tx, ty, nz = courant.shape
    nrec = positions.shape[2]
    steps = amplitudes.shape[1]
    blocks = steps // SNAP
    nh = offsets.shape[0]
    own = nh // ng
    assert ng % 2 == 0 and ty == 2 * ROWS and tx == 2 * HMAX and nz % LANES == 0 and nh % ng == 0 and nx > 1
    assert shots <= 2 and steps % SNAP == 0
    width = tx + (1 if nx == 2 else 2)
    wide = (width + 1) // 2 * 2 * ROWS
    slots = tx + 2 * PAIR
    packs, strips = PAIR + 1, tx // ROWS
    f32, bf16 = jnp.float32, jnp.bfloat16
    dma = pltpu.SemaphoreType.DMA
    vmem = pl.BlockSpec(memory_space=pltpu.VMEM)

    places = positions.transpose(1, 0, 2)
    arguments = (courant, epsilon, delta, checkpoint, places, amplitudes, offsets)

    def held(*shape, dtype=f32):
        return pltpu.VMEM(shape, dtype)

    return pl.pallas_call(
        functools.partial(kernel, sizes),
        out_shape=jax.ShapeDtypeStruct((own, tx, ty, nz), f32),
        in_specs=[pl.BlockSpec(memory_space=pltpu.HBM)] * 7,
        out_specs=vmem,
        scratch_shapes=[
            held(*places.shape, dtype=places.dtype),
            held(*amplitudes.shape),
            pltpu.SMEM(offsets.shape, offsets.dtype),
            held(waves, 2, 2, slots, ROWS, nz),
            held(waves, 2, 2, slots, ROWS, nz),
            held(3, tx, ROWS, nz),
            held(3, slots, ROWS, nz),
            held(3, slots, ROWS, nz),
            held(waves, wide, nrec, dtype=bf16),
            held(waves, wide, nrec, dtype=bf16),
            held(waves, tx * ROWS, nrec, dtype=bf16),
            held(waves, 2 * nrec, nz, dtype=bf16),
            held(waves, wide, nz),
            held(waves, wide, nz),
            held(waves, tx * ROWS, nz),
            held(2, shots, PAIR + 3, ROWS, nz),
            held(2, 3, ROWS, nz),
            held(shots, 2, tx, ROWS, nz),
            held(shots, 2, 2, ROWS, nz),
            held(shots, 2, tx, ROWS, nz),
            held(waves, 2, strips, packs, ROWS, nz),
            held(waves, 2, 2, 1, nz),
            held(2, waves, 2, PAIR + 1, ROWS, nz),
            held(2, waves, 2, strips, packs, ROWS, nz),
            held(2, waves, 2, 2, 1, nz),
            held(blocks, waves, tx + 2 * HMAX, ROWS, nz),
            held(blocks, 2, waves, HMAX, ROWS, nz),
            held(own, tx, ROWS, nz),
            dma((6 + 4 * shots,)),
            dma((2, shots + 1, 4)),
            dma((2, shots + 1, 4)),
            dma((shots, 2)),
            dma((shots, 2)),
            dma((shots, 2, 2)),
            dma((shots, 2, 2)),
            dma((2, waves, 2, 2)),
            dma((2, waves, 2, 2)),
            dma((2, waves, 2, strips)),
            dma((2, waves, 2, strips)),
            dma((2, waves, 2, 2)),
            dma((2, waves, 2, 2)),
            dma((blocks, shots, 2)),
            dma((blocks, shots, 2)),
            dma((2, own)),
            dma((2, own)),
        ],
        compiler_params=pltpu.CompilerParams(
            collective_id=0, has_side_effects=True, vmem_limit_bytes=44 * 1024 * 1024
        ),
    )(*(pltpu.with_memory_space_constraint(v, pltpu.HBM) for v in arguments))


def solution(mesh):
    sizes = tuple(mesh.shape[axis] for axis in ("grp", "gx", "gy"))
    return jax.shard_map(
        functools.partial(shards, sizes),
        mesh=mesh,
        in_specs=(
            P(None, None, None, "gx", "gy", None),
            P("gx", "gy", None),
            P("gx", "gy", None),
            P("gx", "gy", None),
            P(),
            P(),
            P(),
        ),
        out_specs=P("grp", "gx", "gy", None),
        check_vma=False,
    )
```

```python
import functools
import jax
import jax.numpy as jnp
from jax import lax
from jax.experimental import pallas as pl
from jax.experimental.pallas import tpu as pltpu
from jax.sharding import PartitionSpec as P

SNAP = 4
HMAX = 8
PAIR = 2
ROWS = 8
LANES = 128
MESH = pl.DeviceIdType.MESH


def kernel(sizes, courant, epsilon, delta, checkpoint, places, weights, shifts, out,
           positions, amplitudes, offsets, sg, sh, raw, cg, ch, pickg, pickh, pickb, spot, injg, injh, injb, ix, ixc, iy, idg, pi, py, pc, rx, ry, rd,
           snaps, fringe, outgoing,
           ls, isx, irx, isy, iry, isd, ird, hsx, hrx, hsy, hry, hsd, hrd, xs, xr, gs, gr):
    ng, nx, ny = sizes
    shots = checkpoint.shape[0]
    waves = 2 * shots
    tx, ty, nz = courant.shape
    nrec = positions.shape[2]
    steps = amplitudes.shape[1]
    own = offsets.shape[0] // ng
    turns = steps // PAIR
    blocks = steps // SNAP
    per = SNAP // PAIR
    d, a, b = lax.axis_index("grp"), lax.axis_index("gx"), lax.axis_index("gy")
    half = d % 2
    pair = d - half
    other = pair + 1 - half
    flip = b % 2
    hp = half + flip - 2 * half * flip
    partner = {"grp": other, "gx": a, "gy": b}
    width = tx + (1 if nx == 2 else 2)
    lead = a if nx == 2 else 1
    start = PAIR - lead
    right = PAIR + tx
    f32, bf16 = jnp.float32, jnp.bfloat16
    mine = pl.ds(pl.multiple_of(hp * ROWS, ROWS), ROWS)

    inner = (hp, 1 - hp)
    xside = (a > 0, a < nx - 1)
    yside = ((hp == 1) | (b > 0), (hp == 0) | (b < ny - 1))
    near_y = tuple((d + inner[i] * (other - d), b + (2 * i - 1) * (1 - inner[i])) for i in range(2))
    xdev = tuple({"grp": d, "gx": a + 2 * i - 1, "gy": b} for i in range(2))
    ydev = tuple({"grp": near_y[i][0], "gx": a, "gy": near_y[i][1]} for i in range(2))
    corners = [(i, j) for i in range(2) for j in range(2)]
    cthere = {(i, j): xside[i] & yside[j] for i, j in corners}
    cdev = {(i, j): {"grp": near_y[j][0], "gx": a + 2 * i - 1, "gy": near_y[j][1]} for i, j in corners}

    barrier = pltpu.get_barrier_semaphore()
    met = [(xside[i], xdev[i]) for i in range(2)] + [(yside[i], ydev[i]) for i in range(2)]
    met += [(cthere[c], cdev[c]) for c in corners]
    pl.semaphore_signal(barrier, inc=1, device_id=partner, device_id_type=MESH)
    for there, device in met:
        @pl.when(there)
        def _(device=device):
            pl.semaphore_signal(barrier, inc=1, device_id=device, device_id_type=MESH)

    models = (courant, epsilon, delta)

    def model_load(n):
        return pltpu.make_async_copy(models[n].at[:, mine, :], raw.at[n], ls.at[n])

    def state_load(s, moment, field):
        return pltpu.make_async_copy(
            checkpoint.at[s, moment, field, :, mine, :], sg.at[2 * s, moment, field, pl.ds(PAIR, tx)],
            ls.at[3 + 4 * s + 2 * moment + field],
        )

    loads = [(s, moment, field) for s in range(shots) for moment in range(2) for field in range(2)]
    tables = [
        pltpu.make_async_copy(source, target, ls.at[3 + 4 * shots + n])
        for n, (source, target) in enumerate(((places, positions), (weights, amplitudes), (shifts, offsets)))
    ]
    for n in range(3):
        model_load(n).start()
    for load in loads:
        state_load(*load).start()
    for table in tables:
        table.start()

    zero = jnp.zeros((ROWS, nz), f32)
    row = lax.broadcasted_iota(jnp.int32, (ROWS, nz), 0)
    lane = lax.broadcasted_iota(jnp.int32, (ROWS, LANES), 1)
    top, bottom, upper = row == 0, row == ROWS - 1, row < ROWS // 2

    def turn(v, shift, axis=0):
        shift = shift % v.shape[axis]
        return v if shift == 0 else pltpu.roll(v, shift, axis)

    outer = (0, 1, right, right + 1)
    quad, packs, strips = ROWS // PAIR, PAIR + 1, tx // ROWS

    def wipe(x, carry):
        for r in range(waves):
            for moment in range(2):
                for field in range(2):
                    if r % 2:
                        sg[r, moment, field, x] = zero
                    sh[r, moment, field, x] = zero
        return carry

    lax.fori_loop(0, tx + 2 * PAIR, wipe, 0)
    for x in outer:
        for s in range(shots):
            for moment in range(2):
                for field in range(2):
                    sg[2 * s, moment, field, x] = zero
        for n in range(3):
            cg[n, x] = zero
            ch[n, x] = zero
    for side in range(2):
        @pl.when(jnp.logical_not(yside[side]))
        def _(side=side):
            for x in range(tx):
                for s in range(shots):
                    iy[s, side, x] = zero
            for slot in range(2):
                for r in range(waves):
                    for strip in range(strips):
                        for n in range(packs):
                            ry[slot, r, side, strip, n] = zero
    for i, j in corners:
        @pl.when(jnp.logical_not(cthere[i, j]))
        def _(i=i, j=j):
            for s in range(shots):
                idg[s, i, j] = zero
            for slot in range(2):
                for r in range(waves):
                    rd[slot, r, i, j] = zero[:1]

    total = 1
    for there, _ in met:
        total = total + there.astype(jnp.int32)
    pl.semaphore_wait(barrier, total)

    def first_x(side, s, n, arrival=False):
        last = pl.ds(tx - 1 if side else 0, 1)
        into = side if arrival else 1 - side
        if s < shots:
            rows = pl.ds(tx - PAIR if side else 0, PAIR) if n == 0 else last
            source = checkpoint.at[s, n // 2, n % 2, rows, mine, :]
            target = ix.at[into, s, pl.ds(0, PAIR) if n == 0 else pl.ds(n + 1, 1)]
        else:
            source, target = models[n].at[last, mine, :], ixc.at[into, pl.ds(n, 1)]
        return pltpu.make_async_remote_copy(
            src_ref=target if arrival else source, dst_ref=target, send_sem=isx.at[side, s, n],
            recv_sem=irx.at[into, s, n], device_id=xdev[side], device_id_type=MESH,
        )

    firsts = [(shots, n) for n in range(3)] + [(s, n) for s in range(shots) for n in range(4)]
    for side in range(2):
        @pl.when(xside[side])
        def _(side=side):
            for s, n in firsts:
                first_x(side, s, n).start()

    for n in range(3):
        model_load(n).wait()
    for load in loads:
        state_load(*load).wait()

    def first_y(s, side, arrival=False):
        into = side if arrival else 1 - side
        return pltpu.make_async_remote_copy(
            src_ref=iy.at[s, into] if arrival else pi.at[s, side], dst_ref=iy.at[s, into], send_sem=isy.at[s, side],
            recv_sem=iry.at[s, into], device_id=ydev[side], device_id_type=MESH,
        )

    def first_d(s, corner, arrival=False):
        i, j = corner
        u, v = corner if arrival else (1 - i, 1 - j)
        return pltpu.make_async_remote_copy(
            src_ref=idg.at[s, u, v] if arrival else pi.at[s, j, tx - 1 if i else 0], dst_ref=idg.at[s, u, v],
            send_sem=isd.at[s, i, j], recv_sem=ird.at[s, u, v], device_id=cdev[corner], device_id_type=MESH,
        )

    for s in range(shots):
        for x in range(tx):
            tiles = [sg[2 * s, n // 2, n % 2, PAIR + x] for n in range(4)]
            tiles += [raw[n, x] for n in range(3)] if s == 0 else []
            lower = higher = tiles[0]
            for n in range(1, len(tiles)):
                lower = jnp.where(row == n + 1, turn(tiles[n], n + 1), lower)
                higher = jnp.where(row == ROWS - 2 - n, turn(tiles[n], -n - 1), higher)
            pi[s, 0, x] = lower
            pi[s, 1, x] = higher
        for c in corners:
            @pl.when(cthere[c])
            def _(c=c, s=s):
                first_d(s, c).start()
        for side in range(2):
            @pl.when(yside[side])
            def _(side=side, s=s):
                first_y(s, side).start()

    def mix(c, e, v):
        return c + 2.0 * c * e, c * jnp.sqrt(2.0 * v + 1.0), c

    for x in range(tx):
        parts = mix(raw[0, x], raw[1, x], raw[2, x])
        for n in range(3):
            cg[n, PAIR + x] = parts[n]

    for table in tables:
        table.wait()
    tile = 2 * ROWS
    wide = (width * ROWS + tile - 1) // tile
    count = lax.broadcasted_iota(jnp.int32, (tile, nrec), 0)
    level = lax.broadcasted_iota(jnp.int32, (nz, nrec), 0)
    for r in range(waves):
        px = positions[0, r:r + 1, :] - (a * tx - lead)
        qy = positions[1, r:r + 1, :] - (b * ty + hp * ROWS)
        pz = positions[2, r:r + 1, :]
        column = (px >= 0) & (px < width)
        within = (qy >= 0) & (qy < ROWS)
        cell = jnp.where(column & within, px * ROWS + qy, -1)
        brim = jnp.where(column & (qy == ROWS), px * ROWS, jnp.where(column & (qy == -1), px * ROWS + ROWS - 1, -1))
        core = jnp.where((px >= lead) & (px < lead + tx) & within, (px - lead) * ROWS + qy, -1)
        for ref, where, parts in ((pickg, cell, wide), (pickh, brim, wide), (pickb, core, tx * ROWS // tile)):
            for n in range(parts):
                ref[r, pl.ds(n * tile, tile), :] = jnp.where(count + n * tile == where, 1.0, 0.0).astype(bf16)
        where_z = jnp.where(level == pz, 1.0, 0.0).T.astype(bf16)
        spot[r, pl.ds(0, nrec), :] = where_z
        spot[r, pl.ds(nrec, nrec), :] = where_z

    def blank(j, carry):
        for r in range(waves):
            for x in range(HMAX):
                snaps[j, r, x] = zero
                snaps[j, r, HMAX + tx + x] = zero
        return carry

    lax.fori_loop(0, blocks, blank, 0)

    def inject(turn_index, r):
        def strength(moment):
            s = jnp.broadcast_to(amplitudes[r, pl.ds(moment, 1), :], (tile, nrec))
            high = s.astype(bf16)
            low = (s - high.astype(f32)).astype(bf16)
            return high, low

        def weigh(ref, n, parts):
            p = ref[r, pl.ds(n * tile, tile), :]
            return jnp.concatenate([p * parts[0], p * parts[1]], axis=1)

        one, two = strength(PAIR * turn_index), strength(PAIR * turn_index + 1)
        rows = [weigh(pickg, n, one) for n in range(wide)] + [weigh(pickh, n, one) for n in range(wide)]
        rows += [weigh(pickb, n, two) for n in range(tx * ROWS // tile)]
        found = jnp.dot(jnp.concatenate(rows, axis=0), spot[r], preferred_element_type=f32)
        injg[r] = found[:wide * tile]
        injh[r] = found[wide * tile:2 * wide * tile]
        injb[r] = found[2 * wide * tile:]

    def down(v):
        tiles = [v[:, n * LANES:(n + 1) * LANES] for n in range(nz // LANES)]
        fore = [turn(t, 1, 1) for t in tiles]
        back = [turn(t, -1, 1) for t in tiles]
        sums = []
        for n, t in enumerate(tiles):
            before = jnp.where(lane == 0, fore[n - 1] if n else 0.0, fore[n])
            after = jnp.where(lane == LANES - 1, back[n + 1] if n + 1 < len(tiles) else 0.0, back[n])
            sums.append(before + after - 2.0 * t)
        return jnp.concatenate(sums, axis=1)

    def advance(r, now, base, order, brim, gref, href):
        then = 1 - now

        def row_of(w, deep=True):
            slot = base + w
            return [sg[r, now, 0, slot]] + ([sh[r, now, 0, slot]] if deep else [])

        last = None
        for w in order:
            slot = base + w
            if last is not None and w == last + 1:
                behind, here = here, ahead
            else:
                behind, here = row_of(w - 1, brim), row_of(w)
            ahead = row_of(w + 1)
            last = w
            ups, downs = [turn(t, 1) for t in here], [turn(t, -1) for t in here]
            for n in range(2 if brim else 1):
                grid, coefs, source = (sh, ch, href) if n else (sg, cg, gref)
                north = jnp.where(top, ups[1 - n], ups[n])
                south = jnp.where(bottom, downs[1 - n], downs[n])
                m = here[n]
                across = (north + south) + (behind[n] + ahead[n]) - 4.0 * m
                aux = grid[r, now, 1, slot]
                vertical = down(aux)
                extra = source[r, pl.ds(w * ROWS, ROWS), :]
                hor, cpl, ver = (coefs[k, slot] for k in range(3))
                grid[r, then, 0, slot] = 2.0 * m - grid[r, then, 0, slot] + hor * across + cpl * vertical + extra
                grid[r, then, 1, slot] = 2.0 * aux - grid[r, then, 1, slot] + cpl * across + ver * vertical + extra

    def first_merge(s):
        for side in range(2):
            @pl.when(yside[side])
            def _(side=side):
                first_y(s, side, True).wait_recv()
                first_y(s, side).wait_send()
        for c in corners:
            @pl.when(cthere[c])
            def _(c=c):
                first_d(s, c, True).wait_recv()
                first_d(s, c).wait_send()

        for x in range(tx):
            below, above = iy[s, 0, x], iy[s, 1, x]

            def field(n, below=below, above=above):
                if n == 0:
                    return jnp.where(upper, above, below)
                return jnp.where(upper, turn(above, -n - 1), turn(below, n + 1))

            for n in range(4):
                sh[2 * s, n // 2, n % 2, PAIR + x] = field(n)
            if s == 0:
                parts = mix(*(jnp.where(top | bottom, field(4 + n), 0.0) for n in range(3)))
                for n in range(3):
                    ch[n, PAIR + x] = parts[n]
        for side in range(2):
            @pl.when(xside[side])
            def _(side=side):
                for group, n in firsts:
                    if group == s or (s == 0 and group == shots):
                        first_x(side, group, n, True).wait_recv()
                        first_x(side, group, n).wait_send()
                near, low = (right, right) if side else (1, 0)
                for n in range(PAIR):
                    sg[2 * s, 0, 0, low + n] = ix[side, s, n]
                for n in range(1, 4):
                    sg[2 * s, n // 2, n % 2, near] = ix[side, s, n + 1]
                sh[2 * s, 0, 0, near] = jnp.where(upper, idg[s, side, 1], idg[s, side, 0])
                if s == 0:
                    parts = mix(ixc[side, 0], ixc[side, 1], ixc[side, 2])
                    for n in range(3):
                        cg[n, near] = parts[n]

    def halo_x(slot, r, side, n, arrival=False):
        if n == 0:
            rows, target = pl.ds(right - PAIR if side else PAIR, PAIR), pl.ds(0, PAIR)
        else:
            rows, target = pl.ds(right - 1 if side else PAIR, 1), pl.ds(PAIR, 1)
        into = side if arrival else 1 - side
        target = rx.at[slot, r, into, target]
        return pltpu.make_async_remote_copy(
            src_ref=target if arrival else sg.at[r, 0, n, rows], dst_ref=target, send_sem=hsx.at[slot, r, side, n],
            recv_sem=hrx.at[slot, r, into, n], device_id=xdev[side], device_id_type=MESH,
        )

    def halo_y(slot, r, side, strip, arrival=False):
        into = side if arrival else 1 - side
        target = ry.at[slot, r, into, strip]
        return pltpu.make_async_remote_copy(
            src_ref=target if arrival else py.at[r, side, strip], dst_ref=target, send_sem=hsy.at[slot, r, side, strip],
            recv_sem=hry.at[slot, r, into, strip], device_id=ydev[side], device_id_type=MESH,
        )

    def halo_d(slot, r, corner, arrival=False):
        i, j = corner
        u, v = corner if arrival else (1 - i, 1 - j)
        target = rd.at[slot, r, u, v]
        return pltpu.make_async_remote_copy(
            src_ref=target if arrival else pc.at[r, i, j], dst_ref=target,
            send_sem=hsd.at[slot, r, i, j], recv_sem=hrd.at[slot, r, u, v], device_id=cdev[corner],
            device_id_type=MESH,
        )

    def corner(slot, r, side):
        above, below = (jnp.broadcast_to(rd[slot, r, side, n], (ROWS, nz)) for n in (1, 0))
        return jnp.where(upper, above, below)

    def merge(slot, r):
        for side in range(2):
            @pl.when(yside[side])
            def _(side=side):
                for strip in range(strips):
                    halo_y(slot, r, side, strip, True).wait_recv()
                    halo_y(slot, r, side, strip).wait_send()
        for x in range(tx):
            strip, w = x // ROWS, x % ROWS
            n, k = w // quad, w % quad
            below, above = ry[slot, r, 0, strip, n], ry[slot, r, 1, strip, n]
            sh[r, 0, 0, PAIR + x] = jnp.where(upper, turn(above, -PAIR * k), turn(below, -PAIR * (k + 1)))
            below, above = ry[slot, r, 0, strip, PAIR], ry[slot, r, 1, strip, PAIR]
            sh[r, 0, 1, PAIR + x] = jnp.where(upper, turn(above, -w), turn(below, -w - 1))
        for c in corners:
            @pl.when(cthere[c])
            def _(c=c):
                halo_d(slot, r, c, True).wait_recv()
                halo_d(slot, r, c).wait_send()
        for side in range(2):
            @pl.when(xside[side])
            def _(side=side):
                for n in range(2):
                    halo_x(slot, r, side, n, True).wait_recv()
                    halo_x(slot, r, side, n).wait_send()
                near, low = (right, right) if side else (1, 0)
                for n in range(PAIR):
                    sg[r, 0, 0, low + n] = rx[slot, r, side, n]
                sg[r, 0, 1, near] = rx[slot, r, side, PAIR]
                sh[r, 0, 0, near] = corner(slot, r, side)

    def send_x(slot, r):
        for i, j in corners:
            v = sg[r, 0, 0, right - 1 if i else PAIR]
            pc[r, i, j] = v[ROWS - 1:] if j else v[:1]
        for c in corners:
            @pl.when(cthere[c])
            def _(c=c):
                halo_d(slot, r, c).start()
        for side in range(2):
            @pl.when(xside[side])
            def _(side=side):
                for n in range(2):
                    halo_x(slot, r, side, n).start()

    def send_y(slot, r, strip):
        for n in range(packs):
            field, size, first = (0, PAIR, n * quad) if n < PAIR else (1, 1, 0)
            lower = higher = None
            for k in range(ROWS // size):
                v = sg[r, 0, field, PAIR + strip * ROWS + first + k]
                one, two = turn(v, size * k), turn(v, size * (k + 1))
                lower = one if k == 0 else jnp.where(row < size * k, lower, one)
                higher = two if k == 0 else jnp.where(row < size * k, higher, two)
            py[r, 0, strip, n] = lower
            py[r, 1, strip, n] = higher
        for side in range(2):
            @pl.when(yside[side])
            def _(side=side):
                halo_y(slot, r, side, strip).start()

    def fringe_copy(j, s, side, skip, arrival=False):
        into = side if arrival else 1 - side
        both = pl.ds(2 * s, 2)
        target = fringe.at[j, into, both, pl.ds(0, HMAX - skip)]
        source = pl.ds(tx if side else HMAX + skip, HMAX - skip)
        return pltpu.make_async_remote_copy(
            src_ref=target if arrival else snaps.at[j, both, source], dst_ref=target, send_sem=xs.at[j, s, side],
            recv_sem=xr.at[j, s, into], device_id=xdev[side], device_id_type=MESH,
        )

    def send_fringe(j, s, skip):
        for side in range(2):
            @pl.when(xside[side])
            def _(side=side):
                fringe_copy(j, s, side, skip).start()

    def merge_fringe(j, skip):
        for s in range(shots):
            for side in range(2):
                @pl.when(xside[side])
                def _(side=side, s=s):
                    fringe_copy(j, s, side, skip, True).wait_recv()
                    fringe_copy(j, s, side, skip).wait_send()
                    for r in range(2 * s, 2 * s + 2):
                        for x in range(HMAX - skip):
                            snaps[j, r, side * (HMAX + tx + skip) + x] = fringe[j, side, r, x]

    def keep_halo(e, r):
        for side in range(2):
            @pl.when(xside[side])
            def _(side=side):
                for n in range(PAIR):
                    snaps[e // per - 1, r, (HMAX + tx if side else HMAX - PAIR) + n] = rx[e % 2, r, side, n]

    queue = [0, 1] + [r for s in range(1, shots) for r in (2 * s + 1, 2 * s)]
    brink = list(range(PAIR)) + list(range(tx - PAIR, tx))
    rest = [[x for x in range(n * ROWS, (n + 1) * ROWS) if x not in brink] for n in range(strips)]

    def cycle(e, carry):
        for r in range(waves):
            inject(e, r)

        for place, r in enumerate(queue):
            if r % 2 == 0:
                @pl.when(e == 0)
                def _(r=r):
                    first_merge(r // 2)

            @pl.when(e > 0)
            def _(r=r):
                merge(e % 2, r)

            @pl.when((e % per == 0) & (e > 0))
            def _(r=r):
                keep_halo(e, r)

            cut = ROWS + 2
            advance(r, 0, start, range(cut), True, injg, injh)
            advance(r, 1, PAIR, range(ROWS), False, injb, None)

            @pl.when(e < turns - 1)
            def _(r=r):
                send_y((e + 1) % 2, r, 0)

            advance(r, 0, start, range(cut, width), True, injg, injh)
            advance(r, 1, PAIR, range(tx - PAIR, tx), False, injb, None)

            @pl.when(e < turns - 1)
            def _(r=r):
                send_x((e + 1) % 2, r)

            advance(r, 1, PAIR, range(ROWS, tx - PAIR), False, injb, None)

            @pl.when(e < turns - 1)
            def _(r=r):
                send_y((e + 1) % 2, r, 1)

            if place % 2 == 1:
                @pl.when(e % per == per - 1)
                def _(r=r):
                    for n in (r - r % 2, r - r % 2 + 1):
                        for x in range(tx):
                            snaps[e // per, n, HMAX + x] = sg[n, 0, 0, PAIR + x]

                @pl.when(e == turns - 1)
                def _(r=r):
                    send_fringe(blocks - 1, r // 2, 0)

        @pl.when((e % per == per - 1) & (e < turns - 1))
        def _():
            send_fringe(e // per, 0, PAIR)

        @pl.when((e % per == 0) & (e > 0))
        def _():
            for s in range(1, shots):
                send_fringe(e // per - 1, s, PAIR)

        return carry

    lax.fori_loop(0, turns, cycle, 0)

    def swap_copy(n, rows, part):
        return pltpu.make_async_remote_copy(
            src_ref=outgoing.at[n, rows], dst_ref=out.at[n, rows, mine, :], send_sem=gs.at[part, n],
            recv_sem=gr.at[part, n], device_id=partner, device_id_type=MESH,
        )

    def product(shift, x):
        sums = None
        for j in range(blocks):
            for s in range(shots):
                term = snaps[j, 2 * s, HMAX - shift + x] * snaps[j, 2 * s + 1, HMAX + shift + x]
                sums = term if sums is None else sums + term
        return sums

    mid = tx // 2
    spans = [pl.ds(a * mid, mid), pl.ds((1 - a) * mid, mid)] if nx == 2 else [pl.ds(0, mid), pl.ds(mid, mid)]
    for part, rows in enumerate(spans):
        if part == (1 if nx == 2 else 0):
            def earlier(j, carry):
                merge_fringe(j, PAIR)
                return carry

            lax.fori_loop(0, blocks - 1, earlier, 0)
            merge_fringe(blocks - 1, 0)

        def theirs(n, carry, part=part, rows=rows):
            shift = offsets[pair * own + (1 - half) * own + n]
            for x in range(mid):
                outgoing[n, rows.start + x] = product(shift, rows.start + x)
            swap_copy(n, rows, part).start()
            return carry

        lax.fori_loop(0, own, theirs, 0)

    def ours(n, carry):
        shift = offsets[pair * own + half * own + n]
        for x in range(tx):
            out[n, x, mine, :] = product(shift, x)
        return carry

    lax.fori_loop(0, own, ours, 0)
    for part, rows in enumerate(spans):
        def done(n, carry, part=part, rows=rows):
            swap_copy(n, rows, part).wait_recv()
            swap_copy(n, rows, part).wait_send()
            return carry

        lax.fori_loop(0, own, done, 0)


def shards(sizes, checkpoint, courant, epsilon, delta, positions, amplitudes, offsets):
    ng, nx, ny = sizes
    shots = checkpoint.shape[0]
    waves = 2 * shots
    tx, ty, nz = courant.shape
    nrec = positions.shape[2]
    steps = amplitudes.shape[1]
    blocks = steps // SNAP
    nh = offsets.shape[0]
    own = nh // ng
    assert ng % 2 == 0 and ty == 2 * ROWS and tx == 2 * HMAX and nz % LANES == 0 and nh % ng == 0 and nx > 1
    assert shots <= 2 and steps % SNAP == 0
    width = tx + (1 if nx == 2 else 2)
    wide = (width + 1) // 2 * 2 * ROWS
    slots = tx + 2 * PAIR
    packs, strips = PAIR + 1, tx // ROWS
    f32, bf16 = jnp.float32, jnp.bfloat16
    dma = pltpu.SemaphoreType.DMA
    vmem = pl.BlockSpec(memory_space=pltpu.VMEM)

    places = positions.transpose(1, 0, 2)
    arguments = (courant, epsilon, delta, checkpoint, places, amplitudes, offsets)

    def held(*shape, dtype=f32):
        return pltpu.VMEM(shape, dtype)

    return pl.pallas_call(
        functools.partial(kernel, sizes),
        out_shape=jax.ShapeDtypeStruct((own, tx, ty, nz), f32),
        in_specs=[pl.BlockSpec(memory_space=pltpu.HBM)] * 7,
        out_specs=vmem,
        scratch_shapes=[
            held(*places.shape, dtype=places.dtype),
            held(*amplitudes.shape),
            pltpu.SMEM(offsets.shape, offsets.dtype),
            held(waves, 2, 2, slots, ROWS, nz),
            held(waves, 2, 2, slots, ROWS, nz),
            held(3, tx, ROWS, nz),
            held(3, slots, ROWS, nz),
            held(3, slots, ROWS, nz),
            held(waves, wide, nrec, dtype=bf16),
            held(waves, wide, nrec, dtype=bf16),
            held(waves, tx * ROWS, nrec, dtype=bf16),
            held(waves, 2 * nrec, nz, dtype=bf16),
            held(waves, wide, nz),
            held(waves, wide, nz),
            held(waves, tx * ROWS, nz),
            held(2, shots, PAIR + 3, ROWS, nz),
            held(2, 3, ROWS, nz),
            held(shots, 2, tx, ROWS, nz),
            held(shots, 2, 2, ROWS, nz),
            held(shots, 2, tx, ROWS, nz),
            held(waves, 2, strips, packs, ROWS, nz),
            held(waves, 2, 2, 1, nz),
            held(2, waves, 2, PAIR + 1, ROWS, nz),
            held(2, waves, 2, strips, packs, ROWS, nz),
            held(2, waves, 2, 2, 1, nz),
            held(blocks, waves, tx + 2 * HMAX, ROWS, nz),
            held(blocks, 2, waves, HMAX, ROWS, nz),
            held(own, tx, ROWS, nz),
            dma((6 + 4 * shots,)),
            dma((2, shots + 1, 4)),
            dma((2, shots + 1, 4)),
            dma((shots, 2)),
            dma((shots, 2)),
            dma((shots, 2, 2)),
            dma((shots, 2, 2)),
            dma((2, waves, 2, 2)),
            dma((2, waves, 2, 2)),
            dma((2, waves, 2, strips)),
            dma((2, waves, 2, strips)),
            dma((2, waves, 2, 2)),
            dma((2, waves, 2, 2)),
            dma((blocks, shots, 2)),
            dma((blocks, shots, 2)),
            dma((2, own)),
            dma((2, own)),
        ],
        compiler_params=pltpu.CompilerParams(
            collective_id=0, has_side_effects=True, vmem_limit_bytes=44 * 1024 * 1024
        ),
    )(*(pltpu.with_memory_space_constraint(v, pltpu.HBM) for v in arguments))


def solution(mesh):
    sizes = tuple(mesh.shape[axis] for axis in ("grp", "gx", "gy"))
    return jax.shard_map(
        functools.partial(shards, sizes),
        mesh=mesh,
        in_specs=(
            P(None, None, None, "gx", "gy", None),
            P("gx", "gy", None),
            P("gx", "gy", None),
            P("gx", "gy", None),
            P(),
            P(),
            P(),
        ),
        out_specs=P("grp", "gx", "gy", None),
        check_vma=False,
    )
```
